32 devices in a mesh: dp: 8 (over z, y), tensor: 4 (over x, core).
Axes of the slice: x: 2, y: 2, z: 4, core: 2. Of those that a mesh axis runs over, the one named last changes fastest.
Arguments:
- tokens: bfloat16 [16384, 1024], P('dp'), may hold values from -6 to 6
- segment_ids: int32 [16384], P('dp'), may hold values from 0 to 14, as said below
- positions: int32 [16384], P('dp'), may hold values from 0 to 1023, as said below
- pad_mask: int32 [16384], P('dp'), may hold values from 0 to 1, as said below
- w_query: bfloat16 [1024, 1024], P('dp', 'tensor'), may hold values from -0.1875 to 0.1875
- w_key: bfloat16 [1024, 512], P('dp', 'tensor'), may hold values from -0.1875 to 0.1875
- w_value: bfloat16 [1024, 512], P('dp', 'tensor'), may hold values from -0.1875 to 0.1875
- w_out: bfloat16 [1024, 1024], P('tensor', 'dp'), may hold values from -0.75 to 0.75
- w_gate: bfloat16 [1024, 4608], P('dp', 'tensor'), may hold values from -0.1875 to 0.1875
- w_up: bfloat16 [1024, 4608], P('dp', 'tensor'), may hold values from -0.1875 to 0.1875
- w_down: bfloat16 [4608, 1024], P('tensor', 'dp'), may hold values from -0.09375 to 0.09375
- attn_gain: bfloat16 [1024], P('dp'), may hold values from 0.5 to 1.5
- ffn_gain: bfloat16 [1024], P('dp'), may hold values from 0.5 to 1.5
- query_gain: bfloat16 [64], replicated, may hold values from 0.5 to 1.5
- key_gain: bfloat16 [64], replicated, may hold values from 0.5 to 1.5
- cotangent: bfloat16 [16384, 1024], P('dp'), may hold values from -6 to 6
Outputs:
- output: bfloat16 [16384, 1024], P('dp')
- grad_input: float32 [16384, 1024], P('dp')
- grad_query: float32 [1024, 1024], P('dp', 'tensor')
- grad_key: float32 [1024, 512], P('dp', 'tensor')
- grad_value: float32 [1024, 512], P('dp', 'tensor')
- grad_out: float32 [1024, 1024], P('tensor', 'dp')
- grad_gate: float32 [1024, 4608], P('dp', 'tensor')
- grad_up: float32 [1024, 4608], P('dp', 'tensor')
- grad_down: float32 [4608, 1024], P('tensor', 'dp')
- grad_attn_gain: float32 [1024], P('dp')
- grad_ffn_gain: float32 [1024], P('dp')
- grad_query_gain: float32 [64], replicated
- grad_key_gain: float32 [64], replicated
The draws below stay inside these ranges and needn't reach their ends.
Inputs may be any that keep to these rules, and one draw needn't show every extreme that they name: `segment_ids`: within each row of 2048 tokens the numbers never fall; a document holds at most 1024 tokens, and some row holds one of exactly 1024; each row ends with a run of 1 to 128 pads, which form the row's last document and carry the number 8 + 2 * 2048 // 1024 + 2. `positions`: A token's place counted from the start of its document (pads from the start of the pad run). `pad_mask`: each row ends with a run of 1 to 128 pads.
All inputs are finite; a program needn't handle non-finite values.
Results may differ from the reference program's by a relative error of at most 0.02.
Values may be sent and summed in bfloat16 or wider, within the bound.
A program may use at most 256 MiB of HBM per device.

```python
import math
import jax
import jax.numpy as jnp
from jax import lax

D = 1024
H = 16
KV = 8
HD = 64
FF = 4608
ROW_LEN = 2048
SEG_MOST = 1024
PAD_MOST = 128
CUTS = 8
GROUPS = 4
TOKENS = 16384


def packed_layout(key):
    row_count = TOKENS // ROW_LEN
    key_long, key_cut, key_pad, key_pick = jax.random.split(key, 4)
    longest_row = jax.random.randint(key_pick, (), 0, row_count)
    long_len = jax.random.randint(key_long, (row_count,), SEG_MOST // 4, SEG_MOST + 1)
    long_len = jnp.where(jnp.arange(row_count) == longest_row, SEG_MOST, long_len).astype(jnp.int32)
    random_cuts = jax.random.randint(key_cut, (row_count, CUTS), long_len[:, None] + 1, ROW_LEN)
    forced_cuts = long_len[:, None] + SEG_MOST // 2 * jnp.arange(1, 2 * ROW_LEN // SEG_MOST + 1)[None, :]
    cut_points = jnp.concatenate([long_len[:, None], random_cuts, forced_cuts], axis=1).astype(jnp.int32)
    token_place = jnp.arange(ROW_LEN).astype(jnp.int32)
    passed = cut_points[:, None, :] <= token_place[None, :, None]
    segment_rows = jnp.sum(passed.astype(jnp.int32), axis=-1)
    start_rows = jnp.max(jnp.where(passed, cut_points[:, None, :], 0), axis=-1)
    pad_len = jax.random.randint(key_pad, (row_count,), 1, PAD_MOST + 1)
    pad_start = (ROW_LEN - pad_len).astype(jnp.int32)
    is_pad = token_place[None, :] >= pad_start[:, None]
    pad_number = CUTS + 2 * ROW_LEN // SEG_MOST + 2
    segment_rows = jnp.where(is_pad, pad_number, segment_rows)
    start_rows = jnp.where(is_pad, pad_start[:, None], start_rows)
    position_rows = token_place[None, :] - start_rows
    valid_rows = 1 - is_pad.astype(jnp.int32)
    return (segment_rows.reshape(-1).astype(jnp.int32), position_rows.reshape(-1).astype(jnp.int32), valid_rows.reshape(-1).astype(jnp.int32))


def draw_segment_ids(key, part):
    return packed_layout(jax.random.fold_in(key, 17))[0]


def draw_positions(key, part):
    return packed_layout(jax.random.fold_in(key, 17))[1]


def draw_pad_mask(key, part):
    return packed_layout(jax.random.fold_in(key, 17))[2]


def level_of(key, dims, pieces, least, high):
    def one(position, blocks):
        steps = jax.random.uniform(jax.random.fold_in(jax.random.fold_in(key, 6), position), (blocks,), jnp.float32, least / len(pieces), high / len(pieces))
        return jnp.repeat(jnp.exp(steps), dims[position] // blocks).reshape((-1,) + (1,) * (len(dims) - position - 1))

    factor_of = one(*pieces[0])
    for cut in pieces[1:]:
        factor_of = factor_of * one(*cut)
    return factor_of


def bell_draw(stream_key, extent, deviation, bound, pieces=(), kind=jnp.bfloat16):
    values = jax.random.normal(stream_key, extent, jnp.float32) * deviation
    if len(pieces) > 0:
        values = level_of(stream_key, extent, pieces, -0.22, 0.18) * values
    return jnp.clip(values, min=-bound, max=bound).astype(kind)


def setup_inputs(seed: int = 0) -> dict:
    key_list = jax.random.split(jax.random.key(seed), 17)
    tokens = bell_draw(key_list[0], (TOKENS, D), 1.0, 6.0, ((0, 8),))
    segment_ids = draw_segment_ids(jax.random.fold_in(key_list[16], 71), 0)
    positions = draw_positions(jax.random.fold_in(key_list[16], 71), 0)
    pad_mask = draw_pad_mask(jax.random.fold_in(key_list[16], 71), 0)
    w_query = bell_draw(key_list[4], (D, H * HD), D ** -0.5, 0.1875, ((0, 8), (1, 4)))
    w_key = bell_draw(key_list[5], (D, KV * HD), D ** -0.5, 0.1875, ((0, 8), (1, 4)))
    w_value = bell_draw(key_list[6], (D, KV * HD), D ** -0.5, 0.1875, ((0, 8), (1, 4)))
    w_out = bell_draw(key_list[7], (H * HD, D), HD ** -0.5, 0.75, ((0, 4), (1, 8)))
    w_gate = bell_draw(key_list[8], (D, FF), D ** -0.5, 0.1875, ((0, 8), (1, 4)))
    w_up = bell_draw(key_list[9], (D, FF), D ** -0.5, 0.1875, ((0, 8), (1, 4)))
    w_down = bell_draw(key_list[10], (FF, D), FF ** -0.5, 0.09375, ((0, 4), (1, 8)))
    attn_gain = jnp.clip(1.0 + 0.1 * jax.random.normal(key_list[11], (D,), jnp.float32), 0.5, 1.5).astype(jnp.bfloat16)
    ffn_gain = jnp.clip(1.0 + 0.1 * jax.random.normal(key_list[12], (D,), jnp.float32), 0.5, 1.5).astype(jnp.bfloat16)
    query_gain = jnp.clip(1.0 + 0.1 * jax.random.normal(key_list[13], (HD,), jnp.float32), 0.5, 1.5).astype(jnp.bfloat16)
    key_gain = jnp.clip(1.0 + 0.1 * jax.random.normal(key_list[14], (HD,), jnp.float32), 0.5, 1.5).astype(jnp.bfloat16)
    cotangent = bell_draw(key_list[15], (TOKENS, D), 1.0, 6.0, ((0, 8),))
    return {"tokens": tokens, "segment_ids": segment_ids, "positions": positions, "pad_mask": pad_mask, "w_query": w_query, "w_key": w_key, "w_value": w_value, "w_out": w_out, "w_gate": w_gate, "w_up": w_up, "w_down": w_down, "attn_gain": attn_gain, "ffn_gain": ffn_gain, "query_gain": query_gain, "key_gain": key_gain, "cotangent": cotangent}


EPSILON = 1e-05
THETA = 1000000.0
HIGHEST = lax.Precision.HIGHEST

@jax.custom_vjp
def low(v):
    return lax.optimization_barrier(v.astype(jnp.bfloat16)).astype(jnp.float32)

@jax.custom_vjp
def low_back(v):
    return v

def low_keep(v):
    return (low(v), None)

def low_pass(kept, grad):
    return (grad,)

def back_keep(v):
    return (v, None)

def back_low(kept, grad):
    return (low(grad),)
low.defvjp(low_keep, low_pass)
low_back.defvjp(back_keep, back_low)

def rms_norm(values, scales):
    return values * lax.rsqrt(lax.optimization_barrier(jnp.mean(values * values, axis=-1, keepdims=True)) + EPSILON) * scales

def rope_tables(position_ids):
    half_size = HD // 2
    inverse = THETA ** (-(jnp.arange(half_size).astype(jnp.float32) * 2.0 / HD))
    angles = position_ids.astype(jnp.float32)[:, None] * inverse[None, :]
    cos_half = jnp.cos(angles)
    sin_half = jnp.sin(angles)
    return (jnp.concatenate([cos_half, cos_half], axis=-1), jnp.concatenate([sin_half, sin_half], axis=-1))

def rotate(values, cos_table, sin_table):
    half_size = values.shape[-1] // 2
    turned = jnp.concatenate([-values[..., half_size:], values[..., :half_size]], axis=-1)
    return values * cos_table + turned * sin_table

def matmul(left, right):
    return jnp.dot(left, right, precision=HIGHEST, preferred_element_type=jnp.float32)

def layer_row(row_tokens, row_segments, row_positions, row_valid, weights):
    w_query, w_key, w_value, w_out, w_gate, w_up, w_down, attn_gain, ffn_gain, query_gain, key_gain = weights
    seq_len = row_tokens.shape[0]
    token_place = jnp.arange(seq_len)
    same_doc = row_segments[:, None] == row_segments[None, :]
    causal = token_place[None, :] <= token_place[:, None]
    open_key = (row_valid[None, :] == 1) | (token_place[None, :] == token_place[:, None])
    allowed = same_doc & causal & open_key
    cos_table, sin_table = rope_tables(row_positions)
    score_scale = 1.0 / math.sqrt(HD)
    q_group = H // GROUPS
    kv_group = KV // GROUPS
    ff_group = FF // GROUPS
    repeat = q_group // kv_group
    normed_one = low(rms_norm(row_tokens, attn_gain))
    state = row_tokens
    for group_index in range(GROUPS):
        group_input = low_back(normed_one)
        q_cols = slice(group_index * q_group * HD, (group_index + 1) * q_group * HD)
        kv_cols = slice(group_index * kv_group * HD, (group_index + 1) * kv_group * HD)
        raw_query = low_back(matmul(group_input, w_query[:, q_cols])).reshape(seq_len, kv_group, repeat, HD)
        raw_key = low_back(matmul(group_input, w_key[:, kv_cols])).reshape(seq_len, kv_group, HD)
        value_rows = low(low_back(matmul(group_input, w_value[:, kv_cols]))).reshape(seq_len, kv_group, HD)
        query_rot = low(rotate(rms_norm(raw_query, query_gain), cos_table[:, None, None, :], sin_table[:, None, None, :]))
        key_rot = low(rotate(rms_norm(raw_key, key_gain), cos_table[:, None, :], sin_table[:, None, :]))
        scores = low_back(jnp.einsum('qgrd,kgd->grqk', query_rot, key_rot, precision=HIGHEST) * score_scale)
        scores = jnp.where(allowed[None, None], scores, -1e+30)
        soft_weights = jax.nn.softmax(scores, axis=-1)
        heads_out = jnp.einsum('grqk,kgd->qgrd', low(soft_weights), value_rows, precision=HIGHEST)
        heads_out = low(low_back(heads_out)).reshape(seq_len, q_group * HD)
        state = state + low(low_back(matmul(heads_out, w_out[q_cols, :])))
    normed_two = low(rms_norm(state, ffn_gain))
    result = state
    for group_index in range(GROUPS):
        group_input = low_back(normed_two)
        f_cols = slice(group_index * ff_group, (group_index + 1) * ff_group)
        gate_vals = low_back(matmul(group_input, w_gate[:, f_cols]))
        up_vals = low_back(matmul(group_input, w_up[:, f_cols]))
        hidden = low(jax.nn.silu(gate_vals) * up_vals)
        result = result + low(low_back(matmul(hidden, w_down[f_cols, :])))
    return result

def forward(tokens32, segment_ids, positions, pad_mask, weights):
    token_rows = tokens32.reshape(-1, ROW_LEN, D)
    segment_rows = segment_ids.reshape(-1, ROW_LEN)
    position_rows = positions.reshape(-1, ROW_LEN)
    valid_rows = pad_mask.reshape(-1, ROW_LEN)
    row_step = jax.checkpoint(layer_row)

    def scan_step(carry, items):
        return (carry, row_step(items[0], items[1], items[2], items[3], weights))
    carry, outputs = lax.scan(scan_step, jnp.zeros((), jnp.float32), (token_rows, segment_rows, position_rows, valid_rows))
    return outputs.reshape(-1, D)

def reference(tokens, segment_ids, positions, pad_mask, w_query, w_key, w_value, w_out, w_gate, w_up, w_down, attn_gain, ffn_gain, query_gain, key_gain, cotangent):
    weights = [matrix.astype(jnp.float32) for matrix in (w_query, w_key, w_value, w_out, w_gate, w_up, w_down, attn_gain, ffn_gain, query_gain, key_gain)]

    def apply_layer(tokens32, *weight_list):
        return forward(tokens32, segment_ids, positions, pad_mask, weight_list)
    outputs, pullback = jax.vjp(apply_layer, tokens.astype(jnp.float32), *weights)
    grads = pullback(cotangent.astype(jnp.float32))
    return (outputs.astype(jnp.bfloat16), grads[0], grads[1], grads[2], grads[3], grads[4], grads[5], grads[6], grads[7], grads[8], grads[9], grads[10], grads[11])
```

```python
import functools
import math

import jax
import jax.numpy as jnp
from jax import lax
from jax.experimental import pallas as pl
from jax.experimental.pallas import tpu as pltpu
from jax.sharding import PartitionSpec as P

HD = 64
EPSILON = 1e-05
THETA = 1000000.0
BIG_NEGATIVE = -1e30
CHUNKS = 4
BLK = 256
F32 = jnp.float32
BF16 = jnp.bfloat16
SCALE = 1.0 / math.sqrt(HD)
EXP2_SCALE = SCALE * math.log2(math.e)
NT = (((1,), (1,)), ((), ()))
ANY = pl.BlockSpec(memory_space=pl.ANY)


def sds(shape, dtype):
    return jax.ShapeDtypeStruct(shape, dtype)


def whole(shape):
    return pl.BlockSpec(shape, lambda i, *s: (0,) * len(shape))


def dot(left, right):
    return jnp.dot(left, right, preferred_element_type=F32)


def dot_nt(left, right):
    return lax.dot_general(left, right, NT, preferred_element_type=F32)


def cost(micros):
    return pl.CostEstimate(flops=0, bytes_accessed=int(micros * 3.4e6), transcendentals=0)


def after(value, *others):
    return lax.optimization_barrier((value, others))[0]


def params():
    return pltpu.CompilerParams(
        dimension_semantics=("arbitrary",), vmem_limit_bytes=56 * 1024 * 1024
    )


def low_half(shape, period):
    lane = lax.broadcasted_iota(jnp.int32, shape, 1)
    return lax.rem(lane, period) < period // 2


def swap_halves(values):
    left = pltpu.roll(values, 128 - HD // 2, 1)
    right = pltpu.roll(values, HD // 2, 1)
    return jnp.where(low_half(values.shape, HD), left, right)


def pair_mean(values):
    first = low_half(values.shape, 2 * HD)
    low = jnp.sum(jnp.where(first, values, 0.0), axis=1, keepdims=True)
    high = jnp.sum(jnp.where(first, 0.0, values), axis=1, keepdims=True)
    return jnp.where(first, low, high) * (1.0 / HD)


def head_pads(slab, group):
    first = low_half(slab.shape, 2 * HD)
    rolled = pltpu.roll(slab, HD, 1)
    if group == 0:
        pieces = (jnp.where(first, slab, 0.0), jnp.where(first, rolled, 0.0))
    else:
        pieces = (jnp.where(first, 0.0, rolled), jnp.where(first, 0.0, slab))
    return jnp.concatenate(pieces, axis=0).astype(BF16)


def qkv_kernel(
    x_ref, gain_ref, w_ref, cos_ref, sin_ref, qgain_ref, kgain_ref,
    xn_ref, z_ref, q_ref, k_ref, v_ref, kt_ref, vt_ref,
):
    x = x_ref[...].astype(F32)
    rstd = lax.rsqrt(jnp.mean(x * x, axis=1, keepdims=True) + EPSILON)
    xn = (x * rstd * gain_ref[...]).astype(BF16)
    xn_ref[...] = xn
    z = dot(xn, w_ref[...])
    z_ref[...] = z[:, :384]
    cos, sin = cos_ref[...], sin_ref[...]

    def post(values, gain):
        normed = values * lax.rsqrt(pair_mean(values * values) + EPSILON) * gain
        return normed * cos + swap_halves(normed) * sin

    for group in range(2):
        slab = post(z[:, group * 128:(group + 1) * 128], qgain_ref[...])
        q_ref[0, group] = head_pads(slab, group)
    keys = post(z[:, 256:384], kgain_ref[...])
    k_ref[...] = keys.astype(BF16)
    kt_ref[...] = keys.T.astype(BF16)
    values = z[:, 384:512]
    v_ref[...] = values.astype(BF16)
    values_t = values.T.astype(BF16)
    rows = lax.broadcasted_iota(jnp.int32, (16, BLK), 0)
    ones = jnp.where(rows == 0, 1.0, 0.0).astype(BF16)
    for group in range(2):
        vt_ref[group, 0:HD, :] = values_t[group * HD:(group + 1) * HD]
        vt_ref[group, HD:HD + 16, :] = ones


def qkv_call(x, gain, w, cos, sin, qgain, kgain):
    seq, width = x.shape
    blocks = seq // BLK
    row = lambda n: pl.BlockSpec((BLK, n), lambda i: (i, 0))
    return pl.pallas_call(
        qkv_kernel,
        grid=(blocks,),
        in_specs=[
            row(width), whole((1, width)), pl.BlockSpec((width, 512), lambda i: (0, 0)),
            row(128), row(128), whole((1, 128)), whole((1, 128)),
        ],
        out_specs=[
            row(width), row(384),
            pl.BlockSpec((1, 2, 2 * BLK, 128), lambda i: (i, 0, 0, 0)),
            row(128), row(128),
            pl.BlockSpec((128, BLK), lambda i: (0, i)),
            pl.BlockSpec((2, HD + 16, BLK), lambda i: (0, 0, i)),
        ],
        out_shape=[
            sds((seq, width), BF16), sds((seq, 384), F32),
            sds((blocks, 2, 2 * BLK, 128), BF16),
            sds((seq, 128), BF16), sds((seq, 128), BF16),
            sds((128, seq), BF16), sds((2, HD + 16, seq), BF16),
        ],
        compiler_params=params(),
        cost_estimate=cost(12),
        name="qkv",
    )(x, gain, w, cos, sin, qgain, kgain)


class Order:
    def __init__(self, chunk, half, descending):
        self.chunk, self.half, self.descending = chunk, half, descending

    def local(self, i, core):
        half = self.half
        if self.descending:
            return 2 * half - 1 - i
        first = i < half
        base = jnp.where(first, (1 - core) * half, core * half)
        return base + jnp.where(first, i, i - half)

    def block(self, i, core):
        return self.chunk * 2 * self.half + self.local(i, core)

    def is_send(self, i, core):
        if self.descending:
            return jnp.where(core == 0, i < self.half, i >= self.half)
        return i < self.half

    def send(self, i, core):
        half = self.half
        if self.descending:
            return jnp.where(core == 0, jnp.maximum(half - 1 - i, 0), jnp.minimum(half - 1, 2 * half - 1 - i))
        return jnp.minimum(i, half - 1)

    def keep(self, i, core):
        half = self.half
        if self.descending:
            return self.send(i, 1 - core)
        return jnp.maximum(i - half, 0)


def order_specs(order):
    row = lambda n: pl.BlockSpec((BLK, n), lambda i, c, *s: (order.block(i, c[0]), 0))
    local = lambda n: pl.BlockSpec((BLK, n), lambda i, c, *s: (order.local(i, c[0]), 0))
    send = lambda n: pl.BlockSpec((BLK, n), lambda i, c, *s: (order.send(i, c[0]), 0))
    keep = lambda n: pl.BlockSpec((BLK, n), lambda i, c, *s: (order.keep(i, c[0]), 0))
    return row, local, send, keep


def put(is_send, send_ref, keep_ref, value):
    @pl.when(is_send)
    def _():
        send_ref[...] = value

    @pl.when(jnp.logical_not(is_send))
    def _():
        keep_ref[...] = value


def attn_kernel(order, n_prev, core_ref, lo_ref, q_ref, k_ref, vt_ref, start_ref, wo_ref, *rest):
    rest = rest[n_prev:]
    o_ref, lse_ref, send_ref, keep_ref, acc_ref = rest
    i = pl.program_id(0)
    core = core_ref[0]
    block = order.block(i, core)
    start = start_ref[0]
    key_place = lax.broadcasted_iota(jnp.int32, (BLK, 2 * BLK), 0)
    acc_ref[...] = jnp.zeros_like(acc_ref)

    def step(kb, diagonal):
        at = pl.multiple_of(kb * BLK, BLK)
        keys = k_ref[pl.ds(at, BLK), :]
        allowed = key_place >= start - at
        if diagonal:
            lane = lax.broadcasted_iota(jnp.int32, (BLK, 2 * BLK), 1)
            allowed = allowed & (key_place <= lax.rem(lane, BLK))
        for group in range(2):
            scores = dot_nt(keys, q_ref[0, group]) * EXP2_SCALE
            probs = jnp.exp2(jnp.where(allowed, scores, BIG_NEGATIVE)).astype(BF16)
            acc_ref[group] += dot(vt_ref[group, :, pl.ds(at, BLK)], probs)

    def loop_body(kb, carry):
        step(kb, False)
        return carry

    lax.fori_loop(lo_ref[block], block, loop_body, 0)
    step(block, True)
    parts = []
    for group in range(2):
        total = acc_ref[group, HD:HD + 1, :]
        lse_ref[0, group:group + 1, :] = jnp.log2(total)
        heads = acc_ref[group, 0:HD, :] / total
        parts += [heads[:, :BLK], heads[:, BLK:]]
    out = jnp.concatenate(parts, axis=0).T.astype(BF16)
    o_ref[...] = out
    put(order.is_send(i, core), send_ref, keep_ref, dot_nt(out, wo_ref[...]).astype(BF16))


def attn_call(chunk, half, core, lo, q, k, vt, start, w, previous):
    seq = k.shape[0]
    width = w.shape[0]
    blocks = seq // BLK
    order = Order(chunk, half, False)
    row, _, send, keep = order_specs(order)
    n_prev = len(previous)
    by_block = lambda *tail: pl.BlockSpec((1,) + tail, lambda i, c, *s: (order.block(i, c[0]),) + (0,) * len(tail))
    return pl.pallas_call(
        functools.partial(attn_kernel, order, n_prev),
        grid_spec=pltpu.PrefetchScalarGridSpec(
            num_scalar_prefetch=2,
            grid=(2 * half,),
            in_specs=[
                by_block(2, 2 * BLK, 128), whole((seq, 128)), whole((2, HD + 16, seq)),
                by_block(1, 2 * BLK),
                pl.BlockSpec((width, 256), lambda i, *s: (0, 2)),
            ] + [ANY] * n_prev,
            out_specs=[row(256), by_block(2, 2 * BLK), send(width), keep(width)],
            scratch_shapes=[pltpu.VMEM((2, HD + 16, 2 * BLK), F32)],
        ),
        out_shape=[
            sds((seq, 256), BF16), sds((blocks, 2, 2 * BLK), F32),
            sds((half * BLK, width), BF16), sds((half * BLK, width), BF16),
        ],
        input_output_aliases={7 + j: j for j in range(n_prev)},
        compiler_params=params(),
        cost_estimate=cost(3.5 * 2 * half),
        name=f"attn_{chunk}",
    )(core, lo, q, k, vt, start, w, *previous)


def ffn_kernel(order, n_prev, hidden, core_ref, x_ref, own_ref, got_ref, g_ref, gain_ref, w_ref, *rest):
    rest = rest[n_prev:]
    xn_ref, dgu_ref, hid_ref, dsend_ref, dkeep_ref, ysend_ref, ykeep_ref = rest
    i = pl.program_id(0)
    is_send = order.is_send(i, core_ref[0])
    total = jnp.where(is_send, got_ref[...].astype(F32), own_ref[...].astype(F32))
    h = x_ref[...].astype(F32) + total
    rstd = lax.rsqrt(jnp.mean(h * h, axis=1, keepdims=True) + EPSILON)
    xn = (h * rstd * gain_ref[...]).astype(BF16)
    xn_ref[...] = xn
    gate_up = dot(xn, w_ref[:, :2 * hidden])
    gate, up = gate_up[:, :hidden], gate_up[:, hidden:]
    dhid = dot(g_ref[...], w_ref[:, 2 * hidden:])
    sig = 1.0 / (1.0 + jnp.exp(-gate))
    act = gate * sig
    hid = (act * up).astype(BF16)
    hid_ref[...] = hid
    dgate = (dhid * up * (sig * (1.0 + gate * (1.0 - sig)))).astype(BF16)
    dup = (dhid * act).astype(BF16)
    dgu_ref[:, :hidden] = dgate
    dgu_ref[:, hidden:] = dup
    dxn = dot_nt(dgu_ref[...], w_ref[:, :2 * hidden])
    put(is_send, dsend_ref, dkeep_ref, dxn.astype(BF16))
    put(is_send, ysend_ref, ykeep_ref, dot_nt(hid, w_ref[:, 2 * hidden:]).astype(BF16))


def ffn_call(chunk, half, core, x, own, got, g, gain, w, previous, y_previous):
    seq, width = x.shape
    hidden = w.shape[1] // 3
    order = Order(chunk, half, False)
    row, _, send, keep = order_specs(order)
    n_prev = len(previous) + len(y_previous)
    rows = half * BLK
    y_at = (chunk % 2) * half
    y_send = pl.BlockSpec((BLK, width), lambda i, c, *s: (y_at + order.send(i, c[0]), 0))
    y_keep = pl.BlockSpec((BLK, width), lambda i, c, *s: (y_at + order.keep(i, c[0]), 0))
    aliases = {7 + j: j for j in range(len(previous))}
    aliases.update({7 + len(previous) + j: 5 + j for j in range(len(y_previous))})
    return pl.pallas_call(
        functools.partial(ffn_kernel, order, n_prev, hidden),
        grid_spec=pltpu.PrefetchScalarGridSpec(
            num_scalar_prefetch=1,
            grid=(2 * half,),
            in_specs=[
                row(width), keep(width), send(width), row(width), whole((1, width)),
                pl.BlockSpec((width, 3 * hidden), lambda i, *s: (0, 0), pipeline_mode=pl.Buffered(1)),
            ] + [ANY] * n_prev,
            out_specs=[row(width), row(2 * hidden), row(hidden), send(width), keep(width), y_send, y_keep],
        ),
        out_shape=[sds((seq, width), BF16), sds((seq, 2 * hidden), BF16), sds((seq, hidden), BF16)]
        + [sds((rows, width), BF16)] * 2 + [sds((2 * rows, width), BF16)] * 2,
        input_output_aliases=aliases,
        compiler_params=params(),
        cost_estimate=cost(7.5 * 2 * half),
        name=f"ffn_{chunk}",
    )(core, x, own, got, g, gain, w, *previous, *y_previous)


def back_kernel(
    order, n_prev, first, core_ref, lo_ref, x_ref, own_ref, got_ref, down_ref, dgot_ref, g_ref, gain_ref,
    q_ref, k_ref, v_ref, kt_ref, o_ref, lse_ref, start_ref, wo_ref, wqkv_ref, z_ref, cos_ref, sin_ref,
    qgain_ref, kgain_ref, *rest,
):
    carried = () if first else rest[:2]
    rest = rest[n_prev + (0 if first else 2):]
    (dkv_k_ref, dkv_v_ref, dhb_ref, dz_ref, dh_ref, send_ref, keep_ref, fgain_ref, again_ref, hgain_ref,
     do_ref, dq_ref, delta_ref) = rest
    i = pl.program_id(0)
    core = core_ref[0]
    block = order.block(i, core)
    is_send = order.is_send(i, core)

    @pl.when(i == 0)
    def _():
        fgain_ref[...] = jnp.zeros_like(fgain_ref)
        again_ref[...] = jnp.zeros_like(again_ref)
        hgain_ref[...] = jnp.zeros_like(hgain_ref)
        if first:
            dkv_k_ref[...] = jnp.zeros_like(dkv_k_ref)
            dkv_v_ref[...] = jnp.zeros_like(dkv_v_ref)
        else:
            dkv_k_ref[...] = carried[0][...]
            dkv_v_ref[...] = carried[1][...]

    total = jnp.where(is_send, got_ref[...].astype(F32), own_ref[...].astype(F32))
    dxn = jnp.where(is_send, dgot_ref[...].astype(F32), down_ref[...].astype(F32))
    h = x_ref[...].astype(F32) + total
    rstd = lax.rsqrt(jnp.mean(h * h, axis=1, keepdims=True) + EPSILON)
    hhat = h * rstd
    fgain_ref[...] += jnp.sum(dxn * hhat, axis=0, keepdims=True)
    u = dxn * gain_ref[...]
    dh = g_ref[...].astype(F32) + rstd * (u - hhat * jnp.mean(u * hhat, axis=1, keepdims=True))
    dh_ref[...] = dh
    dhb = dh.astype(BF16)
    dhb_ref[...] = dhb
    dheads = dot(dhb, wo_ref[...]).astype(BF16).astype(F32)
    delta_t = (dheads * o_ref[...].astype(F32)).T
    for group in range(2):
        do_ref[group] = head_pads(dheads[:, group * 128:(group + 1) * 128], group)
        sums = [
            jnp.sum(delta_t[(2 * group + r) * HD:(2 * group + r + 1) * HD], axis=0, keepdims=True)
            for r in range(2)
        ]
        delta_ref[group:group + 1, :] = jnp.concatenate(sums, axis=1)
    dq_ref[...] = jnp.zeros_like(dq_ref)
    start = start_ref[0]
    key_place = lax.broadcasted_iota(jnp.int32, (BLK, 2 * BLK), 0)

    def step(kb, diagonal):
        at = pl.multiple_of(kb * BLK, BLK)
        keys = k_ref[pl.ds(at, BLK), :]
        values = v_ref[pl.ds(at, BLK), :]
        allowed = key_place >= start - at
        if diagonal:
            lane = lax.broadcasted_iota(jnp.int32, (BLK, 2 * BLK), 1)
            allowed = allowed & (key_place <= lax.rem(lane, BLK))
        dk = dkv_k_ref[pl.ds(at, BLK), :]
        dv = dkv_v_ref[pl.ds(at, BLK), :]
        for group in range(2):
            queries, douts = q_ref[0, group], do_ref[group]
            scores = dot_nt(keys, queries) * EXP2_SCALE - lse_ref[0, group:group + 1, :]
            probs = jnp.exp2(jnp.where(allowed, scores, BIG_NEGATIVE))
            dprobs = dot_nt(values, douts)
            dscores = (probs * (dprobs - delta_ref[group:group + 1, :])).astype(BF16)
            dv += dot(probs.astype(BF16), douts)
            dk += dot(dscores, queries)
            dq_ref[group] += dot(kt_ref[group * HD:(group + 1) * HD, pl.ds(at, BLK)], dscores)
        dkv_k_ref[pl.ds(at, BLK), :] = dk
        dkv_v_ref[pl.ds(at, BLK), :] = dv

    def loop_body(kb, carry):
        step(kb, False)
        return carry

    lax.fori_loop(lo_ref[block], block, loop_body, 0)
    step(block, True)

    parts = []
    for group in range(2):
        dq_t = dq_ref[group]
        parts += [dq_t[:, :BLK], dq_t[:, BLK:]]
    dq = jnp.concatenate(parts, axis=0).T * SCALE
    cos, sin = cos_ref[...], sin_ref[...]

    def post_back(grad, raw, gain):
        dn = grad * cos - swap_halves(grad) * sin
        rstd = lax.rsqrt(pair_mean(raw * raw) + EPSILON)
        hat = raw * rstd
        gain_grad = jnp.sum(dn * hat, axis=0, keepdims=True)
        dhat = dn * gain
        return rstd * (dhat - hat * pair_mean(dhat * hat)), gain_grad

    at = pl.multiple_of(block * BLK, BLK)
    qg = jnp.zeros((1, 128), F32)
    for group in range(2):
        lanes = slice(group * 128, (group + 1) * 128)
        dzq, gain_grad = post_back(dq[:, lanes], z_ref[:, lanes], qgain_ref[...])
        dz_ref[:, lanes] = dzq.astype(BF16)
        qg += gain_grad
    dzk, kg = post_back(dkv_k_ref[pl.ds(at, BLK), :] * SCALE, z_ref[:, 256:384], kgain_ref[...])
    dz_ref[:, 256:384] = dzk.astype(BF16)
    dz_ref[:, 384:512] = dkv_v_ref[pl.ds(at, BLK), :].astype(BF16)
    hgain_ref[0:1, :] += qg
    hgain_ref[1:2, :] += kg
    dxn_one = dot_nt(dz_ref[...], wqkv_ref[...]).astype(BF16)
    put(is_send, send_ref, keep_ref, dxn_one)
    x = x_ref[...].astype(F32)
    xhat = x * lax.rsqrt(jnp.mean(x * x, axis=1, keepdims=True) + EPSILON)
    again_ref[...] += jnp.sum(dxn_one.astype(F32) * xhat, axis=0, keepdims=True)


def back_call(chunk, half, core, lo, x, own, got, down, dgot, g, gain, q, k, v, kt, o, lse, start, w,
              z, cos, sin, qgain, kgain, carried, previous):
    seq, width = x.shape
    order = Order(chunk, half, True)
    row, local, send, keep = order_specs(order)
    first = len(previous) == 0
    n_prev = len(previous)
    rows = half * BLK
    by_block = lambda *tail: pl.BlockSpec((1,) + tail, lambda i, c, *s: (order.block(i, c[0]),) + (0,) * len(tail))
    n_in = 2 + 21
    extra = [] if first else [whole((seq, 128))] * 2 + [ANY] * n_prev
    return pl.pallas_call(
        functools.partial(back_kernel, order, n_prev, first),
        grid_spec=pltpu.PrefetchScalarGridSpec(
            num_scalar_prefetch=2,
            grid=(2 * half,),
            in_specs=[
                row(width), keep(width), send(width), keep(width), send(width), row(width), whole((1, width)),
                by_block(2, 2 * BLK, 128), whole((seq, 128)), whole((seq, 128)), whole((128, seq)),
                row(256), by_block(2, 2 * BLK), by_block(1, 2 * BLK),
                pl.BlockSpec((width, 256), lambda i, *s: (0, 2)),
                pl.BlockSpec((width, 512), lambda i, *s: (0, 0)),
                row(384), row(128), row(128), whole((1, 128)), whole((1, 128)),
            ] + extra,
            out_specs=[
                whole((seq, 128)), whole((seq, 128)), row(width), row(512), local(width),
                send(width), keep(width), whole((1, width)), whole((1, width)), whole((2, 128)),
            ],
            scratch_shapes=[
                pltpu.VMEM((2, 2 * BLK, 128), BF16),
                pltpu.VMEM((2, HD, 2 * BLK), F32),
                pltpu.VMEM((2, 2 * BLK), F32),
            ],
        ),
        out_shape=[
            sds((seq, 128), F32), sds((seq, 128), F32), sds((seq, width), BF16), sds((seq, 512), BF16),
            sds((2 * rows, width), F32), sds((rows, width), BF16), sds((rows, width), BF16),
            sds((1, width), F32), sds((1, width), F32), sds((2, 128), F32),
        ],
        input_output_aliases={n_in + 2 + j: 2 + j for j in range(n_prev)},
        compiler_params=params(),
        cost_estimate=cost(7.5 * 2 * half),
        name=f"back_{chunk}",
    )(core, lo, x, own, got, down, dgot, g, gain, q, k, v, kt, o, lse, start, w, w, z, cos, sin,
      qgain, kgain, *carried, *previous)


def input_kernel(order, n_prev, core_ref, dh_ref, x_ref, own_ref, got_ref, gain_ref, *rest):
    (out_ref,) = rest[n_prev:]
    i = pl.program_id(0)
    is_send = order.is_send(i, core_ref[0])
    dxn = jnp.where(is_send, got_ref[...].astype(F32), own_ref[...].astype(F32))
    x = x_ref[...].astype(F32)
    rstd = lax.rsqrt(jnp.mean(x * x, axis=1, keepdims=True) + EPSILON)
    xhat = x * rstd
    u = dxn * gain_ref[...]
    out_ref[...] = dh_ref[...] + rstd * (u - xhat * jnp.mean(u * xhat, axis=1, keepdims=True))


def input_call(chunk, half, core, dh, x, own, got, gain, previous):
    seq, width = x.shape
    order = Order(chunk, half, False)
    row, local, send, keep = order_specs(order)
    n_prev = len(previous)
    return pl.pallas_call(
        functools.partial(input_kernel, order, n_prev),
        grid_spec=pltpu.PrefetchScalarGridSpec(
            num_scalar_prefetch=1,
            grid=(2 * half,),
            in_specs=[local(width), row(width), keep(width), send(width), whole((1, width))] + [ANY] * n_prev,
            out_specs=[row(width)],
        ),
        out_shape=[sds((seq, width), F32)],
        input_output_aliases={6 + j: j for j in range(n_prev)},
        compiler_params=params(),
        cost_estimate=cost(2 * 2 * half),
        name=f"grad_input_{chunk}",
    )(core, dh, x, own, got, gain, *previous)


def output_kernel(core_ref, x_ref, *refs):
    (out_ref,) = refs[-1:]
    chunk = pl.program_id(0)
    mine = pl.program_id(1) == core_ref[0]
    for index in range(CHUNKS):
        own_ref, got_ref = refs[2 * index:2 * index + 2]
        yown_ref, ygot_ref = refs[2 * CHUNKS + 2 * (index // 2):2 * CHUNKS + 2 * (index // 2) + 2]
        for kept in range(2):
            @pl.when((chunk == index) & (mine if kept else jnp.logical_not(mine)))
            def _(a_ref=own_ref if kept else got_ref, y_ref=yown_ref if kept else ygot_ref):
                total = a_ref[...].astype(F32) + y_ref[...].astype(F32)
                out_ref[...] = (x_ref[...].astype(F32) + total).astype(BF16)


def output_call(half, core, x, attn_sums, y_sums):
    seq, width = x.shape
    rows = 128
    per = half * BLK // rows
    row = pl.BlockSpec((rows, width), lambda c, h, i, *s: ((c * 2 + h) * per + i, 0))

    def moving(index):
        def at(c, h, i, *s):
            return (jnp.where(c == index, i, jnp.where(c < index, 0, per - 1)), 0)

        return pl.BlockSpec((rows, width), at)

    def y_moving(pair):
        def at(c, h, i, *s):
            here = lax.rem(c, 2) * per + i
            return (jnp.where(c // 2 == pair, here, jnp.where(c // 2 < pair, 0, 2 * per - 1)), 0)

        return pl.BlockSpec((rows, width), at)

    args, specs = [], []
    for index in range(CHUNKS):
        args += list(attn_sums[index])
        specs += [moving(index)] * 2
    for pair in range(CHUNKS // 2):
        args += list(y_sums[pair])
        specs += [y_moving(pair)] * 2
    return pl.pallas_call(
        output_kernel,
        grid_spec=pltpu.PrefetchScalarGridSpec(
            num_scalar_prefetch=1,
            grid=(CHUNKS, 2, per),
            in_specs=[row] + specs,
            out_specs=row,
        ),
        out_shape=sds((seq, width), BF16),
        compiler_params=pltpu.CompilerParams(
            dimension_semantics=("arbitrary",) * 3, vmem_limit_bytes=56 * 1024 * 1024
        ),
        cost_estimate=cost(8),
        name="output",
    )(core, x, *args)


def pack_kernel(wq_ref, wk_ref, wv_ref, wo_ref, gain_ref, wg_ref, wu_ref, wd_ref, attn_ref, ffn_ref):
    queries, keys = wq_ref.shape[1], wk_ref.shape[1]
    hidden = wg_ref.shape[1]
    attn_ref[:, :queries] = wq_ref[...]
    attn_ref[:, queries:queries + keys] = wk_ref[...]
    attn_ref[:, queries + keys:queries + 2 * keys] = wv_ref[...]
    at = queries + 2 * keys
    attn_ref[:, at:at + queries] = wo_ref[...].astype(F32).T.astype(BF16)
    attn_ref[:, at + queries:] = gain_ref[...].astype(F32).T.astype(BF16)
    ffn_ref[:, :hidden] = wg_ref[...]
    ffn_ref[:, hidden:2 * hidden] = wu_ref[...]
    ffn_ref[:, 2 * hidden:] = wd_ref[...].astype(F32).T.astype(BF16)


def pack(w_query, w_key, w_value, w_out, attn_gain, ffn_gain, w_gate, w_up, w_down):
    shard = w_query.shape[0]
    if shard % 128:
        gains = jnp.stack([attn_gain, ffn_gain] + [jnp.zeros_like(attn_gain)] * 126, axis=1)
        return (
            jnp.concatenate([w_query, w_key, w_value, w_out.T, gains], axis=1),
            jnp.concatenate([w_gate, w_up, w_down.T], axis=1),
        )
    gains = jnp.concatenate([attn_gain[None], ffn_gain[None], jnp.zeros((126, shard), BF16)], axis=0)
    columns = 2 * w_query.shape[1] + 2 * w_key.shape[1] + 128
    return pl.pallas_call(
        pack_kernel,
        out_shape=[sds((shard, columns), BF16), sds((shard, 3 * w_gate.shape[1]), BF16)],
        cost_estimate=cost(3),
        name="pack",
    )(w_query, w_key, w_value, w_out, gains, w_gate, w_up, w_down)


def dp_place(n_dp):
    at = lax.axis_index("dp")
    return at // 2, lax.rem(at, 2)


def ring_of(n_dp):
    return [(i, (i + 2) % n_dp) for i in range(n_dp)]


PAIR = [(i, i ^ 1) for i in range(8)]


def place_kernel(at_ref, *refs):
    pieces, out_ref = refs[:8], refs[8]
    i = pl.program_id(0)
    step = lax.rem(at_ref[0] + 4 - i // 2, 4)
    same = lax.rem(i, 2) == at_ref[1]
    for index in range(4):
        for own in range(2):
            @pl.when((step == index) & (same if own else jnp.logical_not(same)))
            def _(ref=pieces[index + 4 * (1 - own)]):
                out_ref[...] = ref[...]


def place_pieces(line, other, z, y):
    rows, columns = line[0].shape
    return pl.pallas_call(
        place_kernel,
        grid_spec=pltpu.PrefetchScalarGridSpec(
            num_scalar_prefetch=1,
            grid=(8,),
            in_specs=[
                pl.BlockSpec((rows, columns), lambda i, *s: (0, 0), pipeline_mode=pl.Buffered(1))
            ] * 8,
            out_specs=pl.BlockSpec((rows, columns), lambda i, *s: (i, 0)),
        ),
        out_shape=sds((8 * rows, columns), line[0].dtype),
        compiler_params=params(),
        cost_estimate=cost(4 * columns / 3456),
        name="place_pieces",
    )(jnp.stack([z, y]).astype(jnp.int32), *line, *other)


class Gather:
    def __init__(self, piece, n_dp):
        self.n_dp, self.piece, self.line, self.other = n_dp, piece, [], []
        if n_dp == 8:
            self.step(piece)

    def step(self, piece):
        self.line.append(piece)
        self.other.append(lax.ppermute(piece, "dp", PAIR))

    def relay(self):
        if self.n_dp == 8:
            self.step(lax.ppermute(self.line[-1], "dp", ring_of(8)))
            return self.line[-1]
        return self.piece

    def result(self):
        if self.n_dp != 8:
            return lax.all_gather(self.piece, "dp", axis=0, tiled=True)
        return place_pieces(self.line, self.other, *dp_place(8))


class Scatter:
    def __init__(self, grad, n_dp):
        self.n_dp = n_dp
        if n_dp != 8:
            self.total = lax.psum_scatter(grad, "dp", scatter_dimension=0, tiled=True).astype(F32)
            return
        z, y = dp_place(n_dp)
        rows, columns = grad.shape[0] // n_dp, grad.shape[1]
        cut = grad.reshape(4, 2, rows, columns)

        def part(step, line):
            return lax.dynamic_slice(
                cut, (lax.rem(z + 4 - step, 4), line, 0, 0), (1, 1, rows, columns)
            ).reshape(rows, columns)

        self.kept = [part(step, y) for step in (1, 2, 3, 4)]
        self.got = [lax.ppermute(part(step, 1 - y), "dp", PAIR) for step in (1, 2, 3, 4)]
        self.total, self.at = None, 0

    def step(self, token):
        if self.n_dp != 8:
            return self.total
        got = after(self.got[self.at], token)
        total = self.kept[self.at].astype(F32) + got.astype(F32)
        if self.total is not None:
            total = total + after(self.total, token).astype(F32)
        self.at += 1
        if self.at == 4:
            self.total = total
            return total
        total = total.astype(BF16)
        self.total = lax.ppermute(total, "dp", ring_of(8))
        return total


def sum_all(value, n_dp):
    for axis, size in (("tensor", 4), ("dp", n_dp)):
        bit = 1
        while bit < size:
            value = value + lax.ppermute(value, axis, [(i, i ^ bit) for i in range(size)])
            bit *= 2
    return value


def body(
    tokens, segment_ids, positions, pad_mask, w_query, w_key, w_value, w_out, w_gate, w_up, w_down,
    attn_gain, ffn_gain, query_gain, key_gain, cotangent,
):
    del segment_ids
    seq, width = tokens.shape
    shard = w_query.shape[0]
    n_dp = width // shard
    hidden = w_gate.shape[1]
    chunks = CHUNKS
    half = seq // chunks // 2 // BLK
    blocks = seq // BLK
    core_id = lax.rem(lax.axis_index("tensor"), 2).astype(jnp.int32).reshape(1)
    near = [(t, t ^ 1) for t in range(4)]
    far = [(t, t ^ 2) for t in range(4)]

    attn_piece, ffn_piece = pack(
        w_query, w_key, w_value, w_out, attn_gain, ffn_gain, w_gate, w_up, w_down
    )
    gather_attn = Gather(attn_piece, n_dp)
    for _ in range(3):
        late = gather_attn.relay()
    w_attn = gather_attn.result()
    gather_ffn = Gather(after(ffn_piece, late), n_dp)
    gain_rows = w_attn[:, 768:770].T.astype(F32)
    attn_scales, ffn_scales = gain_rows[0:1], gain_rows[1:2]
    query_scales = jnp.tile(query_gain.astype(F32), 2)[None]
    key_scales = jnp.tile(key_gain.astype(F32), 2)[None]

    place = jnp.arange(seq, dtype=jnp.int32)
    start = jnp.where(pad_mask == 1, place - positions, place)
    lo = (place[::BLK] - positions[::BLK]) // BLK
    start_rows = jnp.tile(start.reshape(blocks, 1, BLK), (1, 1, 2))
    half_size = HD // 2
    inverse = THETA ** (-(jnp.arange(half_size).astype(F32) * 2.0 / HD))
    angles = positions.astype(F32)[:, None] * inverse[None, :]
    cos_half, sin_half = jnp.cos(angles), jnp.sin(angles)
    cos = jnp.concatenate([cos_half] * 4, axis=1)
    sin = jnp.concatenate([-sin_half, sin_half] * 2, axis=1)

    def pair_sum(send, keep):
        return (keep.astype(F32) + lax.ppermute(send, "tensor", near).astype(F32)).astype(BF16)

    def four_sum(mine):
        own = (mine.astype(F32) + lax.ppermute(mine, "tensor", far).astype(F32)).astype(BF16)
        return own, lax.ppermute(own, "tensor", near)

    xn_one, z, q, k, v, kt, vt = qkv_call(
        tokens, attn_scales, w_attn, cos, sin, query_scales, key_scales
    )
    order = list(range(chunks))[::-1]
    previous = ()
    attn_sum, ffn_grad_sum, input_grad_sum, dhs = {}, {}, {}, {}
    first = gather_ffn.relay()
    pairs = []
    for step, c in enumerate(order):
        turn = after(core_id, first)
        if step >= 2:
            turn = after(turn, pairs[step - 2])
        heads, lse, send, keep = attn_call(c, half, turn, lo, q, k, vt, start_rows, w_attn, previous)
        previous = (heads, lse)
        pairs.append(pair_sum(send, keep))
        attn_sum[c] = four_sum(pairs[-1])
        if step == 1:
            first = gather_ffn.relay()
    gather_ffn.relay()
    w_ffn = gather_ffn.result()
    previous, y_previous = (), ()
    pairs, y_sums = [], {}
    for step, c in enumerate(order):
        own, got = attn_sum[c]
        turn = core_id if step < 2 else after(core_id, pairs[step - 2])
        xn_two, dgu, hid, dsend, dkeep, ysend, ykeep = ffn_call(
            c, half, turn, tokens, own, got, cotangent, ffn_scales, w_ffn, previous, y_previous
        )
        previous = (xn_two, dgu, hid)
        y_previous = (ysend, ykeep) if c % 2 else ()
        pairs.append(pair_sum(dsend, dkeep))
        ffn_grad_sum[c] = four_sum(pairs[-1])
        if c % 2 == 0:
            y_sums[c // 2] = (ysend, ykeep)
    tn = (((0,), (0,)), ((), ()))
    hid = after(hid, pairs[2])
    grad_down_t = lax.dot_general(cotangent, hid, tn, preferred_element_type=F32).astype(BF16)
    dgu = after(dgu, grad_down_t, pairs[3])
    grad_gate_up = lax.dot_general(xn_two, dgu, tn, preferred_element_type=F32).astype(BF16)
    down_scatter = Scatter(grad_down_t, n_dp)
    gate_up_scatter = Scatter(grad_gate_up, n_dp)

    previous, carried = (), ()
    ffn_gain_grad = jnp.zeros((1, width), F32)
    attn_gain_grad = jnp.zeros((1, width), F32)
    head_gain_grad = jnp.zeros((2, 128), F32)
    pairs, before = [], [grad_gate_up]
    y_pairs = {1: y_sums[1], 0: y_sums[0]}
    for step, c in enumerate(order):
        own, got = attn_sum[c]
        down, dgot = ffn_grad_sum[c]
        turn = after(core_id, *before)
        dk, dv, dhb, dz, dhs[c], send, keep, fg, ag, hg = back_call(
            c, half, turn, lo, tokens, own, got, down, dgot, cotangent, ffn_scales, q, k, v, kt,
            heads, lse, start_rows, w_attn, z, cos, sin, query_scales, key_scales, carried, previous,
        )
        carried, previous = (dk, dv), (dhb, dz)
        ffn_gain_grad += fg
        attn_gain_grad += ag
        head_gain_grad += hg
        before = []
        if step < 3:
            before.append(down_scatter.step(hg))
        if 1 <= step < 3:
            before.append(gate_up_scatter.step(hg))
        if step == 0:
            ysend, ykeep = y_sums[1]
            y_sums[1] = four_sum(pair_sum(after(ysend, hg), ykeep))
        if step == 1:
            ysend, ykeep = y_sums[0]
            y_sums[0] = four_sum(pair_sum(after(ysend, hg), ykeep))
        if step >= 1:
            before.append(pairs[-1])
        pairs.append(pair_sum(send, keep))
        input_grad_sum[c] = four_sum(pairs[-1])

    dz = after(dz, *before)
    grad_qkv = lax.dot_general(xn_one, dz, tn, preferred_element_type=F32).astype(BF16)
    grad_out_t = lax.dot_general(dhb, heads, tn, preferred_element_type=F32).astype(BF16)
    grad_attn = jnp.concatenate([grad_qkv, grad_out_t], axis=1)
    attn_scatter = Scatter(grad_attn, n_dp)
    head_gains = head_gain_grad[:, :HD] + head_gain_grad[:, HD:]
    small = jnp.concatenate(
        [attn_gain_grad.reshape(-1), 0.25 * ffn_gain_grad.reshape(-1), head_gains.reshape(-1)]
    )
    small = sum_all(small.reshape(-1, 128), n_dp).reshape(-1)
    mine = lax.axis_index("dp") * shard
    grad_attn_gain = lax.dynamic_slice(small, (mine,), (shard,))
    grad_ffn_gain = lax.dynamic_slice(small, (width + mine,), (shard,))
    down_own = down_scatter.step(grad_attn)
    for _ in range(2):
        gate_up_own = gate_up_scatter.step(grad_attn)
    for _ in range(4):
        attn_own = attn_scatter.step(grad_attn)

    previous_in = ()
    for c in order:
        eown, egot = input_grad_sum[c]
        (grad_input,) = input_call(c, half, core_id, dhs[c], tokens, eown, egot, attn_scales, previous_in)
        previous_in = (grad_input,)
    output = output_call(half, core_id, tokens, attn_sum, y_sums)
    return (
        output,
        grad_input,
        attn_own[:, :256],
        attn_own[:, 256:384],
        attn_own[:, 384:512],
        attn_own[:, 512:768].T,
        gate_up_own[:, :hidden],
        gate_up_own[:, hidden:],
        down_own.T,
        grad_attn_gain,
        grad_ffn_gain,
        small[2 * width:2 * width + HD],
        small[2 * width + HD:],
    )


def solution(mesh):
    rows, flat, both = P("dp", None), P("dp"), P("dp", "tensor")
    columns = P("tensor", "dp")
    return jax.shard_map(
        body,
        mesh=mesh,
        in_specs=(
            rows, flat, flat, flat, both, both, both, columns, both, both, columns, flat, flat, P(), P(), rows,
        ),
        out_specs=(rows, rows, both, both, both, columns, both, both, columns, flat, flat, P(), P()),
        check_vma=False,
    )
```

```python
import functools
import math

import jax
import jax.numpy as jnp
from jax import lax
from jax.experimental import pallas as pl
from jax.experimental.pallas import tpu as pltpu
from jax.sharding import PartitionSpec as P

HD = 64
EPSILON = 1e-05
THETA = 1000000.0
BIG_NEGATIVE = -1e30
CHUNKS = 4
BLK = 256
F32 = jnp.float32
BF16 = jnp.bfloat16
SCALE = 1.0 / math.sqrt(HD)
EXP2_SCALE = SCALE * math.log2(math.e)
NT = (((1,), (1,)), ((), ()))
ANY = pl.BlockSpec(memory_space=pl.ANY)


def sds(shape, dtype):
    return jax.ShapeDtypeStruct(shape, dtype)


def whole(shape):
    return pl.BlockSpec(shape, lambda i, *s: (0,) * len(shape))


def dot(left, right):
    return jnp.dot(left, right, preferred_element_type=F32)


def dot_nt(left, right):
    return lax.dot_general(left, right, NT, preferred_element_type=F32)


def cost(micros):
    return pl.CostEstimate(flops=0, bytes_accessed=int(micros * 3.4e6), transcendentals=0)


def after(value, *others):
    return lax.optimization_barrier((value, others))[0]


def params():
    return pltpu.CompilerParams(
        dimension_semantics=("arbitrary",), vmem_limit_bytes=56 * 1024 * 1024
    )


def low_half(shape, period):
    lane = lax.broadcasted_iota(jnp.int32, shape, 1)
    return lax.rem(lane, period) < period // 2


def swap_halves(values):
    left = pltpu.roll(values, 128 - HD // 2, 1)
    right = pltpu.roll(values, HD // 2, 1)
    return jnp.where(low_half(values.shape, HD), left, right)


def pair_mean(values):
    first = low_half(values.shape, 2 * HD)
    low = jnp.sum(jnp.where(first, values, 0.0), axis=1, keepdims=True)
    high = jnp.sum(jnp.where(first, 0.0, values), axis=1, keepdims=True)
    return jnp.where(first, low, high) * (1.0 / HD)


def head_pads(slab, group):
    first = low_half(slab.shape, 2 * HD)
    rolled = pltpu.roll(slab, HD, 1)
    if group == 0:
        pieces = (jnp.where(first, slab, 0.0), jnp.where(first, rolled, 0.0))
    else:
        pieces = (jnp.where(first, 0.0, rolled), jnp.where(first, 0.0, slab))
    return jnp.concatenate(pieces, axis=0).astype(BF16)


def qkv_kernel(
    x_ref, gain_ref, w_ref, cos_ref, sin_ref, qgain_ref, kgain_ref,
    xn_ref, z_ref, q_ref, k_ref, v_ref, kt_ref, vt_ref,
):
    x = x_ref[...].astype(F32)
    rstd = lax.rsqrt(jnp.mean(x * x, axis=1, keepdims=True) + EPSILON)
    xn = (x * rstd * gain_ref[...]).astype(BF16)
    xn_ref[...] = xn
    z = dot(xn, w_ref[...])
    z_ref[...] = z[:, :384]
    cos, sin = cos_ref[...], sin_ref[...]

    def post(values, gain):
        normed = values * lax.rsqrt(pair_mean(values * values) + EPSILON) * gain
        return normed * cos + swap_halves(normed) * sin

    for group in range(2):
        slab = post(z[:, group * 128:(group + 1) * 128], qgain_ref[...])
        q_ref[0, group] = head_pads(slab, group)
    keys = post(z[:, 256:384], kgain_ref[...])
    k_ref[...] = keys.astype(BF16)
    kt_ref[...] = keys.T.astype(BF16)
    values = z[:, 384:512]
    v_ref[...] = values.astype(BF16)
    values_t = values.T.astype(BF16)
    rows = lax.broadcasted_iota(jnp.int32, (16, BLK), 0)
    ones = jnp.where(rows == 0, 1.0, 0.0).astype(BF16)
    for group in range(2):
        vt_ref[group, 0:HD, :] = values_t[group * HD:(group + 1) * HD]
        vt_ref[group, HD:HD + 16, :] = ones


def qkv_call(x, gain, w, cos, sin, qgain, kgain):
    seq, width = x.shape
    blocks = seq // BLK
    row = lambda n: pl.BlockSpec((BLK, n), lambda i: (i, 0))
    return pl.pallas_call(
        qkv_kernel,
        grid=(blocks,),
        in_specs=[
            row(width), whole((1, width)), pl.BlockSpec((width, 512), lambda i: (0, 0)),
            row(128), row(128), whole((1, 128)), whole((1, 128)),
        ],
        out_specs=[
            row(width), row(384),
            pl.BlockSpec((1, 2, 2 * BLK, 128), lambda i: (i, 0, 0, 0)),
            row(128), row(128),
            pl.BlockSpec((128, BLK), lambda i: (0, i)),
            pl.BlockSpec((2, HD + 16, BLK), lambda i: (0, 0, i)),
        ],
        out_shape=[
            sds((seq, width), BF16), sds((seq, 384), F32),
            sds((blocks, 2, 2 * BLK, 128), BF16),
            sds((seq, 128), BF16), sds((seq, 128), BF16),
            sds((128, seq), BF16), sds((2, HD + 16, seq), BF16),
        ],
        compiler_params=params(),
        cost_estimate=cost(0.6),
        name="qkv",
    )(x, gain, w, cos, sin, qgain, kgain)


class Order:
    def __init__(self, chunk, half, descending):
        self.chunk, self.half, self.descending = chunk, half, descending

    def local(self, i, core):
        half = self.half
        if self.descending:
            return 2 * half - 1 - i
        first = i < half
        base = jnp.where(first, (1 - core) * half, core * half)
        return base + jnp.where(first, i, i - half)

    def block(self, i, core):
        return self.chunk * 2 * self.half + self.local(i, core)

    def is_send(self, i, core):
        if self.descending:
            return jnp.where(core == 0, i < self.half, i >= self.half)
        return i < self.half

    def send(self, i, core):
        half = self.half
        if self.descending:
            return jnp.where(core == 0, jnp.maximum(half - 1 - i, 0), jnp.minimum(half - 1, 2 * half - 1 - i))
        return jnp.minimum(i, half - 1)

    def keep(self, i, core):
        half = self.half
        if self.descending:
            return self.send(i, 1 - core)
        return jnp.maximum(i - half, 0)


def order_specs(order):
    row = lambda n: pl.BlockSpec((BLK, n), lambda i, c, *s: (order.block(i, c[0]), 0))
    local = lambda n: pl.BlockSpec((BLK, n), lambda i, c, *s: (order.local(i, c[0]), 0))
    send = lambda n: pl.BlockSpec((BLK, n), lambda i, c, *s: (order.send(i, c[0]), 0))
    keep = lambda n: pl.BlockSpec((BLK, n), lambda i, c, *s: (order.keep(i, c[0]), 0))
    return row, local, send, keep


def put(is_send, send_ref, keep_ref, value):
    @pl.when(is_send)
    def _():
        send_ref[...] = value

    @pl.when(jnp.logical_not(is_send))
    def _():
        keep_ref[...] = value


def attn_kernel(order, n_prev, core_ref, lo_ref, q_ref, k_ref, vt_ref, start_ref, wo_ref, *rest):
    rest = rest[n_prev:]
    o_ref, lse_ref, send_ref, keep_ref, acc_ref = rest
    i = pl.program_id(0)
    core = core_ref[0]
    block = order.block(i, core)
    start = start_ref[0]
    key_place = lax.broadcasted_iota(jnp.int32, (BLK, 2 * BLK), 0)
    acc_ref[...] = jnp.zeros_like(acc_ref)

    def step(kb, diagonal):
        at = pl.multiple_of(kb * BLK, BLK)
        keys = k_ref[pl.ds(at, BLK), :]
        allowed = key_place >= start - at
        if diagonal:
            lane = lax.broadcasted_iota(jnp.int32, (BLK, 2 * BLK), 1)
            allowed = allowed & (key_place <= lax.rem(lane, BLK))
        for group in range(2):
            scores = dot_nt(keys, q_ref[0, group]) * EXP2_SCALE
            probs = jnp.exp2(jnp.where(allowed, scores, BIG_NEGATIVE)).astype(BF16)
            acc_ref[group] += dot(vt_ref[group, :, pl.ds(at, BLK)], probs)

    def loop_body(kb, carry):
        step(kb, False)
        return carry

    lax.fori_loop(lo_ref[block], block, loop_body, 0)
    step(block, True)
    parts = []
    for group in range(2):
        total = acc_ref[group, HD:HD + 1, :]
        lse_ref[0, group:group + 1, :] = jnp.log2(total)
        heads = acc_ref[group, 0:HD, :] / total
        parts += [heads[:, :BLK], heads[:, BLK:]]
    out = jnp.concatenate(parts, axis=0).T.astype(BF16)
    o_ref[...] = out
    put(order.is_send(i, core), send_ref, keep_ref, dot_nt(out, wo_ref[...]).astype(BF16))


def attn_call(chunk, half, core, lo, q, k, vt, start, w, previous):
    seq = k.shape[0]
    width = w.shape[0]
    blocks = seq // BLK
    order = Order(chunk, half, False)
    row, _, send, keep = order_specs(order)
    n_prev = len(previous)
    by_block = lambda *tail: pl.BlockSpec((1,) + tail, lambda i, c, *s: (order.block(i, c[0]),) + (0,) * len(tail))
    return pl.pallas_call(
        functools.partial(attn_kernel, order, n_prev),
        grid_spec=pltpu.PrefetchScalarGridSpec(
            num_scalar_prefetch=2,
            grid=(2 * half,),
            in_specs=[
                by_block(2, 2 * BLK, 128), whole((seq, 128)), whole((2, HD + 16, seq)),
                by_block(1, 2 * BLK),
                pl.BlockSpec((width, 256), lambda i, *s: (0, 2)),
            ] + [ANY] * n_prev,
            out_specs=[row(256), by_block(2, 2 * BLK), send(width), keep(width)],
            scratch_shapes=[pltpu.VMEM((2, HD + 16, 2 * BLK), F32)],
        ),
        out_shape=[
            sds((seq, 256), BF16), sds((blocks, 2, 2 * BLK), F32),
            sds((half * BLK, width), BF16), sds((half * BLK, width), BF16),
        ],
        input_output_aliases={7 + j: j for j in range(n_prev)},
        compiler_params=params(),
        cost_estimate=cost(0.2 * 2 * half),
        name=f"attn_{chunk}",
    )(core, lo, q, k, vt, start, w, *previous)


def ffn_kernel(order, n_prev, hidden, core_ref, x_ref, own_ref, got_ref, g_ref, gain_ref, w_ref, *rest):
    rest = rest[n_prev:]
    xn_ref, dgu_ref, hid_ref, dsend_ref, dkeep_ref, ysend_ref, ykeep_ref = rest
    i = pl.program_id(0)
    is_send = order.is_send(i, core_ref[0])
    total = jnp.where(is_send, got_ref[...].astype(F32), own_ref[...].astype(F32))
    h = x_ref[...].astype(F32) + total
    rstd = lax.rsqrt(jnp.mean(h * h, axis=1, keepdims=True) + EPSILON)
    xn = (h * rstd * gain_ref[...]).astype(BF16)
    xn_ref[...] = xn
    gate_up = dot(xn, w_ref[:, :2 * hidden])
    gate, up = gate_up[:, :hidden], gate_up[:, hidden:]
    dhid = dot(g_ref[...], w_ref[:, 2 * hidden:])
    sig = 1.0 / (1.0 + jnp.exp(-gate))
    act = gate * sig
    hid = (act * up).astype(BF16)
    hid_ref[...] = hid
    dgate = (dhid * up * (sig * (1.0 + gate * (1.0 - sig)))).astype(BF16)
    dup = (dhid * act).astype(BF16)
    dgu_ref[:, :hidden] = dgate
    dgu_ref[:, hidden:] = dup
    dxn = dot_nt(dgu_ref[...], w_ref[:, :2 * hidden])
    put(is_send, dsend_ref, dkeep_ref, dxn.astype(BF16))
    put(is_send, ysend_ref, ykeep_ref, dot_nt(hid, w_ref[:, 2 * hidden:]).astype(BF16))


def ffn_call(chunk, half, core, x, own, got, g, gain, w, previous, y_previous):
    seq, width = x.shape
    hidden = w.shape[1] // 3
    order = Order(chunk, half, False)
    row, _, send, keep = order_specs(order)
    n_prev = len(previous) + len(y_previous)
    rows = half * BLK
    y_at = (chunk % 2) * half
    y_send = pl.BlockSpec((BLK, width), lambda i, c, *s: (y_at + order.send(i, c[0]), 0))
    y_keep = pl.BlockSpec((BLK, width), lambda i, c, *s: (y_at + order.keep(i, c[0]), 0))
    aliases = {7 + j: j for j in range(len(previous))}
    aliases.update({7 + len(previous) + j: 5 + j for j in range(len(y_previous))})
    return pl.pallas_call(
        functools.partial(ffn_kernel, order, n_prev, hidden),
        grid_spec=pltpu.PrefetchScalarGridSpec(
            num_scalar_prefetch=1,
            grid=(2 * half,),
            in_specs=[
                row(width), keep(width), send(width), row(width), whole((1, width)),
                pl.BlockSpec((width, 3 * hidden), lambda i, *s: (0, 0), pipeline_mode=pl.Buffered(1)),
            ] + [ANY] * n_prev,
            out_specs=[row(width), row(2 * hidden), row(hidden), send(width), keep(width), y_send, y_keep],
        ),
        out_shape=[sds((seq, width), BF16), sds((seq, 2 * hidden), BF16), sds((seq, hidden), BF16)]
        + [sds((rows, width), BF16)] * 2 + [sds((2 * rows, width), BF16)] * 2,
        input_output_aliases=aliases,
        compiler_params=params(),
        cost_estimate=cost(5 * 7.5 * 2 * half),
        name=f"ffn_{chunk}",
    )(core, x, own, got, g, gain, w, *previous, *y_previous)


def back_kernel(
    order, n_prev, first, core_ref, lo_ref, x_ref, own_ref, got_ref, down_ref, dgot_ref, g_ref, gain_ref,
    q_ref, k_ref, v_ref, kt_ref, o_ref, lse_ref, start_ref, wo_ref, wqkv_ref, z_ref, cos_ref, sin_ref,
    qgain_ref, kgain_ref, *rest,
):
    carried = () if first else rest[:2]
    rest = rest[n_prev + (0 if first else 2):]
    (dkv_k_ref, dkv_v_ref, dhb_ref, dz_ref, dh_ref, send_ref, keep_ref, fgain_ref, again_ref, hgain_ref,
     do_ref, dq_ref, delta_ref) = rest
    i = pl.program_id(0)
    core = core_ref[0]
    block = order.block(i, core)
    is_send = order.is_send(i, core)

    @pl.when(i == 0)
    def _():
        fgain_ref[...] = jnp.zeros_like(fgain_ref)
        again_ref[...] = jnp.zeros_like(again_ref)
        hgain_ref[...] = jnp.zeros_like(hgain_ref)
        if first:
            dkv_k_ref[...] = jnp.zeros_like(dkv_k_ref)
            dkv_v_ref[...] = jnp.zeros_like(dkv_v_ref)
        else:
            dkv_k_ref[...] = carried[0][...]
            dkv_v_ref[...] = carried[1][...]

    total = jnp.where(is_send, got_ref[...].astype(F32), own_ref[...].astype(F32))
    dxn = jnp.where(is_send, dgot_ref[...].astype(F32), down_ref[...].astype(F32))
    h = x_ref[...].astype(F32) + total
    rstd = lax.rsqrt(jnp.mean(h * h, axis=1, keepdims=True) + EPSILON)
    hhat = h * rstd
    fgain_ref[...] += jnp.sum(dxn * hhat, axis=0, keepdims=True)
    u = dxn * gain_ref[...]
    dh = g_ref[...].astype(F32) + rstd * (u - hhat * jnp.mean(u * hhat, axis=1, keepdims=True))
    dh_ref[...] = dh
    dhb = dh.astype(BF16)
    dhb_ref[...] = dhb
    dheads = dot(dhb, wo_ref[...]).astype(BF16).astype(F32)
    delta_t = (dheads * o_ref[...].astype(F32)).T
    for group in range(2):
        do_ref[group] = head_pads(dheads[:, group * 128:(group + 1) * 128], group)
        sums = [
            jnp.sum(delta_t[(2 * group + r) * HD:(2 * group + r + 1) * HD], axis=0, keepdims=True)
            for r in range(2)
        ]
        delta_ref[group:group + 1, :] = jnp.concatenate(sums, axis=1)
    dq_ref[...] = jnp.zeros_like(dq_ref)
    start = start_ref[0]
    key_place = lax.broadcasted_iota(jnp.int32, (BLK, 2 * BLK), 0)

    def step(kb, diagonal):
        at = pl.multiple_of(kb * BLK, BLK)
        keys = k_ref[pl.ds(at, BLK), :]
        values = v_ref[pl.ds(at, BLK), :]
        allowed = key_place >= start - at
        if diagonal:
            lane = lax.broadcasted_iota(jnp.int32, (BLK, 2 * BLK), 1)
            allowed = allowed & (key_place <= lax.rem(lane, BLK))
        dk = dkv_k_ref[pl.ds(at, BLK), :]
        dv = dkv_v_ref[pl.ds(at, BLK), :]
        for group in range(2):
            queries, douts = q_ref[0, group], do_ref[group]
            scores = dot_nt(keys, queries) * EXP2_SCALE - lse_ref[0, group:group + 1, :]
            probs = jnp.exp2(jnp.where(allowed, scores, BIG_NEGATIVE))
            dprobs = dot_nt(values, douts)
            dscores = (probs * (dprobs - delta_ref[group:group + 1, :])).astype(BF16)
            dv += dot(probs.astype(BF16), douts)
            dk += dot(dscores, queries)
            dq_ref[group] += dot(kt_ref[group * HD:(group + 1) * HD, pl.ds(at, BLK)], dscores)
        dkv_k_ref[pl.ds(at, BLK), :] = dk
        dkv_v_ref[pl.ds(at, BLK), :] = dv

    def loop_body(kb, carry):
        step(kb, False)
        return carry

    lax.fori_loop(lo_ref[block], block, loop_body, 0)
    step(block, True)

    parts = []
    for group in range(2):
        dq_t = dq_ref[group]
        parts += [dq_t[:, :BLK], dq_t[:, BLK:]]
    dq = jnp.concatenate(parts, axis=0).T * SCALE
    cos, sin = cos_ref[...], sin_ref[...]

    def post_back(grad, raw, gain):
        dn = grad * cos - swap_halves(grad) * sin
        rstd = lax.rsqrt(pair_mean(raw * raw) + EPSILON)
        hat = raw * rstd
        gain_grad = jnp.sum(dn * hat, axis=0, keepdims=True)
        dhat = dn * gain
        return rstd * (dhat - hat * pair_mean(dhat * hat)), gain_grad

    at = pl.multiple_of(block * BLK, BLK)
    qg = jnp.zeros((1, 128), F32)
    for group in range(2):
        lanes = slice(group * 128, (group + 1) * 128)
        dzq, gain_grad = post_back(dq[:, lanes], z_ref[:, lanes], qgain_ref[...])
        dz_ref[:, lanes] = dzq.astype(BF16)
        qg += gain_grad
    dzk, kg = post_back(dkv_k_ref[pl.ds(at, BLK), :] * SCALE, z_ref[:, 256:384], kgain_ref[...])
    dz_ref[:, 256:384] = dzk.astype(BF16)
    dz_ref[:, 384:512] = dkv_v_ref[pl.ds(at, BLK), :].astype(BF16)
    hgain_ref[0:1, :] += qg
    hgain_ref[1:2, :] += kg
    dxn_one = dot_nt(dz_ref[...], wqkv_ref[...]).astype(BF16)
    put(is_send, send_ref, keep_ref, dxn_one)
    x = x_ref[...].astype(F32)
    xhat = x * lax.rsqrt(jnp.mean(x * x, axis=1, keepdims=True) + EPSILON)
    again_ref[...] += jnp.sum(dxn_one.astype(F32) * xhat, axis=0, keepdims=True)


def back_call(chunk, half, core, lo, x, own, got, down, dgot, g, gain, q, k, v, kt, o, lse, start, w,
              z, cos, sin, qgain, kgain, carried, previous):
    seq, width = x.shape
    order = Order(chunk, half, True)
    row, local, send, keep = order_specs(order)
    first = len(previous) == 0
    n_prev = len(previous)
    rows = half * BLK
    by_block = lambda *tail: pl.BlockSpec((1,) + tail, lambda i, c, *s: (order.block(i, c[0]),) + (0,) * len(tail))
    n_in = 2 + 21
    extra = [] if first else [whole((seq, 128))] * 2 + [ANY] * n_prev
    return pl.pallas_call(
        functools.partial(back_kernel, order, n_prev, first),
        grid_spec=pltpu.PrefetchScalarGridSpec(
            num_scalar_prefetch=2,
            grid=(2 * half,),
            in_specs=[
                row(width), keep(width), send(width), keep(width), send(width), row(width), whole((1, width)),
                by_block(2, 2 * BLK, 128), whole((seq, 128)), whole((seq, 128)), whole((128, seq)),
                row(256), by_block(2, 2 * BLK), by_block(1, 2 * BLK),
                pl.BlockSpec((width, 256), lambda i, *s: (0, 2)),
                pl.BlockSpec((width, 512), lambda i, *s: (0, 0)),
                row(384), row(128), row(128), whole((1, 128)), whole((1, 128)),
            ] + extra,
            out_specs=[
                whole((seq, 128)), whole((seq, 128)), row(width), row(512), local(width),
                send(width), keep(width), whole((1, width)), whole((1, width)), whole((2, 128)),
            ],
            scratch_shapes=[
                pltpu.VMEM((2, 2 * BLK, 128), BF16),
                pltpu.VMEM((2, HD, 2 * BLK), F32),
                pltpu.VMEM((2, 2 * BLK), F32),
            ],
        ),
        out_shape=[
            sds((seq, 128), F32), sds((seq, 128), F32), sds((seq, width), BF16), sds((seq, 512), BF16),
            sds((2 * rows, width), F32), sds((rows, width), BF16), sds((rows, width), BF16),
            sds((1, width), F32), sds((1, width), F32), sds((2, 128), F32),
        ],
        input_output_aliases={n_in + 2 + j: 2 + j for j in range(n_prev)},
        compiler_params=params(),
        cost_estimate=cost(5 * 7.5 * 2 * half),
        name=f"back_{chunk}",
    )(core, lo, x, own, got, down, dgot, g, gain, q, k, v, kt, o, lse, start, w, w, z, cos, sin,
      qgain, kgain, *carried, *previous)


def input_kernel(order, n_prev, core_ref, dh_ref, x_ref, own_ref, got_ref, gain_ref, *rest):
    (out_ref,) = rest[n_prev:]
    i = pl.program_id(0)
    is_send = order.is_send(i, core_ref[0])
    dxn = jnp.where(is_send, got_ref[...].astype(F32), own_ref[...].astype(F32))
    x = x_ref[...].astype(F32)
    rstd = lax.rsqrt(jnp.mean(x * x, axis=1, keepdims=True) + EPSILON)
    xhat = x * rstd
    u = dxn * gain_ref[...]
    out_ref[...] = dh_ref[...] + rstd * (u - xhat * jnp.mean(u * xhat, axis=1, keepdims=True))


def input_call(chunk, half, core, dh, x, own, got, gain, previous):
    seq, width = x.shape
    order = Order(chunk, half, False)
    row, local, send, keep = order_specs(order)
    n_prev = len(previous)
    return pl.pallas_call(
        functools.partial(input_kernel, order, n_prev),
        grid_spec=pltpu.PrefetchScalarGridSpec(
            num_scalar_prefetch=1,
            grid=(2 * half,),
            in_specs=[local(width), row(width), keep(width), send(width), whole((1, width))] + [ANY] * n_prev,
            out_specs=[row(width)],
        ),
        out_shape=[sds((seq, width), F32)],
        input_output_aliases={6 + j: j for j in range(n_prev)},
        compiler_params=params(),
        cost_estimate=cost(5 * 2 * 2 * half),
        name=f"grad_input_{chunk}",
    )(core, dh, x, own, got, gain, *previous)


def output_kernel(core_ref, x_ref, *refs):
    (out_ref,) = refs[-1:]
    chunk = pl.program_id(0)
    mine = pl.program_id(1) == core_ref[0]
    for index in range(CHUNKS):
        own_ref, got_ref = refs[2 * index:2 * index + 2]
        yown_ref, ygot_ref = refs[2 * CHUNKS + 2 * (index // 2):2 * CHUNKS + 2 * (index // 2) + 2]
        for kept in range(2):
            @pl.when((chunk == index) & (mine if kept else jnp.logical_not(mine)))
            def _(a_ref=own_ref if kept else got_ref, y_ref=yown_ref if kept else ygot_ref):
                total = a_ref[...].astype(F32) + y_ref[...].astype(F32)
                out_ref[...] = (x_ref[...].astype(F32) + total).astype(BF16)


def output_call(half, core, x, attn_sums, y_sums):
    seq, width = x.shape
    rows = BLK
    per = half * BLK // rows
    row = pl.BlockSpec((rows, width), lambda c, h, i, *s: ((c * 2 + h) * per + i, 0))

    def moving(index):
        def at(c, h, i, *s):
            return (jnp.where(c == index, i, jnp.where(c < index, 0, per - 1)), 0)

        return pl.BlockSpec((rows, width), at)

    def y_moving(pair):
        def at(c, h, i, *s):
            here = lax.rem(c, 2) * per + i
            return (jnp.where(c // 2 == pair, here, jnp.where(c // 2 < pair, 0, 2 * per - 1)), 0)

        return pl.BlockSpec((rows, width), at)

    args, specs = [], []
    for index in range(CHUNKS):
        args += list(attn_sums[index])
        specs += [moving(index)] * 2
    for pair in range(CHUNKS // 2):
        args += list(y_sums[pair])
        specs += [y_moving(pair)] * 2
    return pl.pallas_call(
        output_kernel,
        grid_spec=pltpu.PrefetchScalarGridSpec(
            num_scalar_prefetch=1,
            grid=(CHUNKS, 2, per),
            in_specs=[row] + specs,
            out_specs=row,
        ),
        out_shape=sds((seq, width), BF16),
        compiler_params=pltpu.CompilerParams(
            dimension_semantics=("arbitrary",) * 3, vmem_limit_bytes=56 * 1024 * 1024
        ),
        cost_estimate=cost(5 * 8),
        name="output",
    )(core, x, *args)


def pack_kernel(wq_ref, wk_ref, wv_ref, wo_ref, gain_ref, wg_ref, wu_ref, wd_ref, attn_ref, ffn_ref):
    queries, keys = wq_ref.shape[1], wk_ref.shape[1]
    hidden = wg_ref.shape[1]
    attn_ref[:, :queries] = wq_ref[...]
    attn_ref[:, queries:queries + keys] = wk_ref[...]
    attn_ref[:, queries + keys:queries + 2 * keys] = wv_ref[...]
    at = queries + 2 * keys
    attn_ref[:, at:at + queries] = wo_ref[...].astype(F32).T.astype(BF16)
    attn_ref[:, at + queries:] = gain_ref[...].astype(F32).T.astype(BF16)
    ffn_ref[:, :hidden] = wg_ref[...]
    ffn_ref[:, hidden:2 * hidden] = wu_ref[...]
    ffn_ref[:, 2 * hidden:] = wd_ref[...].astype(F32).T.astype(BF16)


def pack(w_query, w_key, w_value, w_out, attn_gain, ffn_gain, w_gate, w_up, w_down):
    shard = w_query.shape[0]
    if shard % 128:
        gains = jnp.stack([attn_gain, ffn_gain] + [jnp.zeros_like(attn_gain)] * 126, axis=1)
        return (
            jnp.concatenate([w_query, w_key, w_value, w_out.T, gains], axis=1),
            jnp.concatenate([w_gate, w_up, w_down.T], axis=1),
        )
    gains = jnp.concatenate([attn_gain[None], ffn_gain[None], jnp.zeros((126, shard), BF16)], axis=0)
    columns = 2 * w_query.shape[1] + 2 * w_key.shape[1] + 128
    return pl.pallas_call(
        pack_kernel,
        out_shape=[sds((shard, columns), BF16), sds((shard, 3 * w_gate.shape[1]), BF16)],
        cost_estimate=cost(3),
        name="pack",
    )(w_query, w_key, w_value, w_out, gains, w_gate, w_up, w_down)


def dp_place(n_dp):
    at = lax.axis_index("dp")
    return at // 2, lax.rem(at, 2)


def ring_of(n_dp):
    return [(i, (i + 2) % n_dp) for i in range(n_dp)]


PAIR = [(i, i ^ 1) for i in range(8)]


def place_kernel(at_ref, *refs):
    pieces, out_ref = refs[:8], refs[8]
    i = pl.program_id(0)
    step = lax.rem(at_ref[0] + 4 - i // 2, 4)
    same = lax.rem(i, 2) == at_ref[1]
    for index in range(4):
        for own in range(2):
            @pl.when((step == index) & (same if own else jnp.logical_not(same)))
            def _(ref=pieces[index + 4 * (1 - own)]):
                out_ref[...] = ref[...]


def place_pieces(line, other, z, y):
    rows, columns = line[0].shape
    return pl.pallas_call(
        place_kernel,
        grid_spec=pltpu.PrefetchScalarGridSpec(
            num_scalar_prefetch=1,
            grid=(8,),
            in_specs=[
                pl.BlockSpec((rows, columns), lambda i, *s: (0, 0), pipeline_mode=pl.Buffered(1))
            ] * 8,
            out_specs=pl.BlockSpec((rows, columns), lambda i, *s: (i, 0)),
        ),
        out_shape=sds((8 * rows, columns), line[0].dtype),
        compiler_params=params(),
        cost_estimate=cost(0.2),
        name="place_pieces",
    )(jnp.stack([z, y]).astype(jnp.int32), *line, *other)


class Gather:
    def __init__(self, piece, n_dp, *clear):
        self.n_dp, self.piece, self.line, self.other = n_dp, piece, [], []
        if n_dp == 8:
            self.step(piece, *clear)

    def step(self, piece, *clear):
        self.line.append(piece)
        self.other.append(lax.ppermute(after(piece, *clear) if clear else piece, "dp", PAIR))

    def relay(self):
        if self.n_dp == 8:
            piece = self.line[-1]
            if len(self.line) > 1:
                piece = after(piece, self.other[-2])
            self.step(lax.ppermute(piece, "dp", ring_of(8)))
            return self.line[-1]
        return self.piece

    def crossed(self, at):
        return self.other[at] if self.n_dp == 8 else self.piece

    def result(self):
        if self.n_dp != 8:
            return lax.all_gather(self.piece, "dp", axis=0, tiled=True)
        return place_pieces(self.line, self.other, *dp_place(8))


class Scatter:
    def __init__(self, grad, n_dp):
        self.n_dp = n_dp
        if n_dp != 8:
            self.total = lax.psum_scatter(grad, "dp", scatter_dimension=0, tiled=True).astype(F32)
            self.got = [self.total] * 4
            return
        z, y = dp_place(n_dp)
        rows, columns = grad.shape[0] // n_dp, grad.shape[1]

        def part(step, line):
            at = (lax.rem(z + 4 - step, 4) * 2 + line) * rows
            return lax.dynamic_slice(grad, (at, 0), (rows, columns))

        self.kept = [part(step, y) for step in (1, 2, 3, 4)]
        self.got = [lax.ppermute(part(step, 1 - y), "dp", PAIR) for step in (1, 2, 3, 4)]
        self.total, self.at = None, 0

    def step(self, token):
        if self.n_dp != 8:
            return self.total
        got = after(self.got[self.at], token)
        total = self.kept[self.at].astype(F32) + got.astype(F32)
        if self.total is not None:
            total = total + after(self.total, token).astype(F32)
        self.at += 1
        if self.at == 4:
            self.total = total
            return total
        total = total.astype(BF16)
        self.total = lax.ppermute(total, "dp", ring_of(8))
        return total


def sum_all(value, n_dp):
    for axis, size in (("tensor", 4), ("dp", n_dp)):
        bit = 1
        while bit < size:
            value = value + lax.ppermute(value, axis, [(i, i ^ bit) for i in range(size)])
            bit *= 2
    return value


def body(
    tokens, segment_ids, positions, pad_mask, w_query, w_key, w_value, w_out, w_gate, w_up, w_down,
    attn_gain, ffn_gain, query_gain, key_gain, cotangent,
):
    del segment_ids
    seq, width = tokens.shape
    shard = w_query.shape[0]
    n_dp = width // shard
    hidden = w_gate.shape[1]
    chunks = CHUNKS
    half = seq // chunks // 2 // BLK
    blocks = seq // BLK
    core_id = lax.rem(lax.axis_index("tensor"), 2).astype(jnp.int32).reshape(1)
    near = [(t, t ^ 1) for t in range(4)]
    far = [(t, t ^ 2) for t in range(4)]

    attn_piece, ffn_piece = pack(
        w_query, w_key, w_value, w_out, attn_gain, ffn_gain, w_gate, w_up, w_down
    )
    gather_attn = Gather(attn_piece, n_dp)
    for _ in range(3):
        late = gather_attn.relay()
    w_attn = gather_attn.result()
    gather_ffn = Gather(after(ffn_piece, late), n_dp, *gather_attn.other)
    gain_rows = w_attn[:, 768:770].T.astype(F32)
    attn_scales, ffn_scales = gain_rows[0:1], gain_rows[1:2]
    query_scales = jnp.tile(query_gain.astype(F32), 2)[None]
    key_scales = jnp.tile(key_gain.astype(F32), 2)[None]

    place = jnp.arange(seq, dtype=jnp.int32)
    start = jnp.where(pad_mask == 1, place - positions, place)
    lo = (place[::BLK] - positions[::BLK]) // BLK
    start_rows = jnp.tile(start.reshape(blocks, 1, BLK), (1, 1, 2))
    half_size = HD // 2
    inverse = THETA ** (-(jnp.arange(half_size).astype(F32) * 2.0 / HD))
    angles = positions.astype(F32)[:, None] * inverse[None, :]
    cos_half, sin_half = jnp.cos(angles), jnp.sin(angles)
    cos = jnp.concatenate([cos_half] * 4, axis=1)
    sin = jnp.concatenate([-sin_half, sin_half] * 2, axis=1)

    def pair_sum(send, keep):
        return (keep.astype(F32) + lax.ppermute(send, "tensor", near).astype(F32)).astype(BF16)

    def four_sum(mine):
        own = (mine.astype(F32) + lax.ppermute(mine, "tensor", far).astype(F32)).astype(BF16)
        return own, lax.ppermute(own, "tensor", near)

    line_one = gather_ffn.relay()
    xn_one, z, q, k, v, kt, vt = qkv_call(
        tokens, attn_scales, w_attn, cos, sin, query_scales, key_scales
    )
    order = list(range(chunks))[::-1]
    previous = ()
    attn_sum, ffn_grad_sum, input_grad_sum, dhs = {}, {}, {}, {}
    pairs = []
    for step, c in enumerate(order):
        turn = core_id
        if step == 0:
            turn = after(turn, line_one, gather_ffn.crossed(0))
            line_two = gather_ffn.relay()
        if step == 2:
            turn = after(turn, pairs[0], line_two, gather_ffn.crossed(1))
            gather_ffn.relay()
        if step == 3:
            turn = after(turn, pairs[1])
        heads, lse, send, keep = attn_call(c, half, turn, lo, q, k, vt, start_rows, w_attn, previous)
        previous = (heads, lse)
        pairs.append(pair_sum(send, keep))
        attn_sum[c] = four_sum(pairs[-1])
    w_ffn = gather_ffn.result()
    previous, y_previous = (), ()
    pairs, y_sums, y_pairs = [], {}, {}
    for step, c in enumerate(order):
        own, got = attn_sum[c]
        turn = core_id
        if step == 0:
            turn = after(turn, attn_sum[order[1]], attn_sum[order[2]][0])
        if step == 1:
            turn = after(turn, attn_sum[order[3]][0])
        if step >= 2:
            turn = after(turn, pairs[step - 2])
        if step == 3:
            turn = after(turn, ffn_grad_sum[order[0]][0])
        xn_two, dgu, hid, dsend, dkeep, ysend, ykeep = ffn_call(
            c, half, turn, tokens, own, got, cotangent, ffn_scales, w_ffn, previous, y_previous
        )
        previous = (xn_two, dgu, hid)
        y_previous = (ysend, ykeep) if c % 2 else ()
        pairs.append(pair_sum(dsend, dkeep))
        ffn_grad_sum[c] = four_sum(pairs[-1])
        if c % 2 == 0:
            y_pairs[c // 2] = pair_sum(ysend, ykeep)
    tn = (((0,), (0,)), ((), ()))
    hid = after(hid, pairs[2], ffn_grad_sum[order[1]][0], y_pairs[1])
    grad_down_t = lax.dot_general(cotangent, hid, tn, preferred_element_type=F32).astype(BF16)
    dgu = after(dgu, grad_down_t, pairs[3], ffn_grad_sum[order[2]][0], ffn_grad_sum[order[0]][1], y_pairs[0])
    grad_gate_up = lax.dot_general(xn_two, dgu, tn, preferred_element_type=F32).astype(BF16)
    down_scatter = Scatter(grad_down_t, n_dp)
    gate_up_scatter = Scatter(grad_gate_up, n_dp)

    previous, carried = (), ()
    ffn_gain_grad = jnp.zeros((1, width), F32)
    attn_gain_grad = jnp.zeros((1, width), F32)
    head_gain_grad = jnp.zeros((2, 128), F32)
    pairs = []
    before = [down_scatter.step(grad_gate_up), down_scatter.got[:3], ffn_grad_sum[order[3]][0]]
    for step, c in enumerate(order):
        own, got = attn_sum[c]
        down, dgot = ffn_grad_sum[c]
        turn = after(core_id, *before)
        dk, dv, dhb, dz, dhs[c], send, keep, fg, ag, hg = back_call(
            c, half, turn, lo, tokens, own, got, down, dgot, cotangent, ffn_scales, q, k, v, kt,
            heads, lse, start_rows, w_attn, z, cos, sin, query_scales, key_scales, carried, previous,
        )
        carried, previous = (dk, dv), (dhb, dz)
        ffn_gain_grad += fg
        attn_gain_grad += ag
        head_gain_grad += hg
        before = [gate_up_scatter.step(hg), down_scatter.got[3]]
        if step < 3:
            before.append(down_scatter.step(hg))
        if step == 0:
            y_sums[1] = four_sum(y_pairs[1])
            before.append(y_sums[1][0])
        if step == 1:
            y_sums[0] = four_sum(y_pairs[0])
            before.append((y_sums[0][0], y_sums[1][1]))
        if step >= 1:
            before.append(pairs[step - 1])
        if step >= 2:
            before.append(input_grad_sum[order[step - 2]][0])
        if step >= 3:
            before.append((input_grad_sum[order[step - 3]][1], y_sums[0][1]))
        pairs.append(pair_sum(send, keep))
        input_grad_sum[c] = four_sum(pairs[-1])
    down_own, gate_up_own = down_scatter.total, gate_up_scatter.total

    dz = after(dz, *before)
    grad_qkv = lax.dot_general(xn_one, dz, tn, preferred_element_type=F32).astype(BF16)
    grad_out_t = lax.dot_general(dhb, heads, tn, preferred_element_type=F32).astype(BF16)
    grad_attn = jnp.concatenate([grad_qkv, grad_out_t], axis=1)
    attn_scatter = Scatter(grad_attn, n_dp)
    head_gains = head_gain_grad[:, :HD] + head_gain_grad[:, HD:]
    small = jnp.concatenate(
        [attn_gain_grad.reshape(-1), 0.25 * ffn_gain_grad.reshape(-1), head_gains.reshape(-1)]
    )
    sent = attn_scatter.step(grad_attn)
    small = sum_all(after(small, sent).reshape(-1, 128), n_dp).reshape(-1)
    mine = lax.axis_index("dp") * shard
    grad_attn_gain = lax.dynamic_slice(small, (mine,), (shard,))
    grad_ffn_gain = lax.dynamic_slice(small, (width + mine,), (shard,))
    output = output_call(half, after(core_id, grad_attn), tokens, attn_sum, y_sums)
    previous_in = ()
    for step, c in enumerate(order):
        eown, egot = input_grad_sum[c]
        turn = after(core_id, sent, output, attn_scatter.got) if step == 0 else core_id
        (grad_input,) = input_call(c, half, turn, dhs[c], tokens, eown, egot, attn_scales, previous_in)
        previous_in = (grad_input,)
        if step == 0:
            sent = attn_scatter.step(grad_attn)
        if step == 2:
            sent = attn_scatter.step(grad_attn)
    attn_own = attn_scatter.step(grad_attn)
    return (
        output,
        grad_input,
        attn_own[:, :256],
        attn_own[:, 256:384],
        attn_own[:, 384:512],
        attn_own[:, 512:768].T,
        gate_up_own[:, :hidden],
        gate_up_own[:, hidden:],
        down_own.T,
        grad_attn_gain,
        grad_ffn_gain,
        small[2 * width:2 * width + HD],
        small[2 * width + HD:],
    )


def solution(mesh):
    rows, flat, both = P("dp", None), P("dp"), P("dp", "tensor")
    columns = P("tensor", "dp")
    return jax.shard_map(
        body,
        mesh=mesh,
        in_specs=(
            rows, flat, flat, flat, both, both, both, columns, both, both, columns, flat, flat, P(), P(), rows,
        ),
        out_specs=(rows, rows, both, both, both, columns, both, both, columns, flat, flat, P(), P()),
        check_vma=False,
    )
```

```python
import functools
import math

import jax
import jax.numpy as jnp
from jax import lax
from jax.experimental import pallas as pl
from jax.experimental.pallas import tpu as pltpu
from jax.sharding import PartitionSpec as P

HD = 64
EPSILON = 1e-05
THETA = 1000000.0
BIG_NEGATIVE = -1e30
CHUNKS = 4
BLK = 256
F32 = jnp.float32
BF16 = jnp.bfloat16
SCALE = 1.0 / math.sqrt(HD)
EXP2_SCALE = SCALE * math.log2(math.e)
NT = (((1,), (1,)), ((), ()))
ANY = pl.BlockSpec(memory_space=pl.ANY)


def sds(shape, dtype):
    return jax.ShapeDtypeStruct(shape, dtype)


def whole(shape):
    return pl.BlockSpec(shape, lambda i, *s: (0,) * len(shape))


def dot(left, right):
    return jnp.dot(left, right, preferred_element_type=F32)


def dot_nt(left, right):
    return lax.dot_general(left, right, NT, preferred_element_type=F32)


def cost(micros):
    return pl.CostEstimate(flops=0, bytes_accessed=int(micros * 3.4e6), transcendentals=0)


def after(value, *others):
    return lax.optimization_barrier((value, others))[0]


def params():
    return pltpu.CompilerParams(
        dimension_semantics=("arbitrary",), vmem_limit_bytes=56 * 1024 * 1024
    )


def low_half(shape, period):
    lane = lax.broadcasted_iota(jnp.int32, shape, 1)
    return lax.rem(lane, period) < period // 2


def swap_halves(values):
    left = pltpu.roll(values, 128 - HD // 2, 1)
    right = pltpu.roll(values, HD // 2, 1)
    return jnp.where(low_half(values.shape, HD), left, right)


def pair_mean(values):
    first = low_half(values.shape, 2 * HD)
    low = jnp.sum(jnp.where(first, values, 0.0), axis=1, keepdims=True)
    high = jnp.sum(jnp.where(first, 0.0, values), axis=1, keepdims=True)
    return jnp.where(first, low, high) * (1.0 / HD)


def head_pads(slab, group):
    first = low_half(slab.shape, 2 * HD)
    rolled = pltpu.roll(slab, HD, 1)
    if group == 0:
        pieces = (jnp.where(first, slab, 0.0), jnp.where(first, rolled, 0.0))
    else:
        pieces = (jnp.where(first, 0.0, rolled), jnp.where(first, 0.0, slab))
    return jnp.concatenate(pieces, axis=0).astype(BF16)


def qkv_kernel(
    x_ref, gain_ref, w_ref, cos_ref, sin_ref, qgain_ref, kgain_ref,
    xn_ref, z_ref, q_ref, k_ref, v_ref, kt_ref, vt_ref,
):
    x = x_ref[...].astype(F32)
    rstd = lax.rsqrt(jnp.mean(x * x, axis=1, keepdims=True) + EPSILON)
    xn = (x * rstd * gain_ref[...]).astype(BF16)
    xn_ref[...] = xn
    z = dot(xn, w_ref[...])
    z_ref[...] = z[:, :384]
    cos, sin = cos_ref[...], sin_ref[...]

    def post(values, gain):
        normed = values * lax.rsqrt(pair_mean(values * values) + EPSILON) * gain
        return normed * cos + swap_halves(normed) * sin

    for group in range(2):
        slab = post(z[:, group * 128:(group + 1) * 128], qgain_ref[...])
        q_ref[0, group] = head_pads(slab, group)
    keys = post(z[:, 256:384], kgain_ref[...])
    k_ref[...] = keys.astype(BF16)
    kt_ref[...] = keys.T.astype(BF16)
    values = z[:, 384:512]
    v_ref[...] = values.astype(BF16)
    values_t = values.T.astype(BF16)
    rows = lax.broadcasted_iota(jnp.int32, (16, BLK), 0)
    ones = jnp.where(rows == 0, 1.0, 0.0).astype(BF16)
    for group in range(2):
        vt_ref[group, 0:HD, :] = values_t[group * HD:(group + 1) * HD]
        vt_ref[group, HD:HD + 16, :] = ones


def qkv_call(x, gain, w, cos, sin, qgain, kgain):
    seq, width = x.shape
    blocks = seq // BLK
    row = lambda n: pl.BlockSpec((BLK, n), lambda i: (i, 0))
    return pl.pallas_call(
        qkv_kernel,
        grid=(blocks,),
        in_specs=[
            row(width), whole((1, width)), pl.BlockSpec((width, 512), lambda i: (0, 0)),
            row(128), row(128), whole((1, 128)), whole((1, 128)),
        ],
        out_specs=[
            row(width), row(384),
            pl.BlockSpec((1, 2, 2 * BLK, 128), lambda i: (i, 0, 0, 0)),
            row(128), row(128),
            pl.BlockSpec((128, BLK), lambda i: (0, i)),
            pl.BlockSpec((2, HD + 16, BLK), lambda i: (0, 0, i)),
        ],
        out_shape=[
            sds((seq, width), BF16), sds((seq, 384), F32),
            sds((blocks, 2, 2 * BLK, 128), BF16),
            sds((seq, 128), BF16), sds((seq, 128), BF16),
            sds((128, seq), BF16), sds((2, HD + 16, seq), BF16),
        ],
        compiler_params=params(),
        cost_estimate=cost(0.6),
        name="qkv",
    )(x, gain, w, cos, sin, qgain, kgain)


class Order:
    def __init__(self, chunk, half, descending):
        self.chunk, self.half, self.descending = chunk, half, descending

    def local(self, i, core):
        half = self.half
        if self.descending:
            return 2 * half - 1 - i
        first = i < half
        base = jnp.where(first, (1 - core) * half, core * half)
        return base + jnp.where(first, i, i - half)

    def block(self, i, core):
        return self.chunk * 2 * self.half + self.local(i, core)

    def is_send(self, i, core):
        if self.descending:
            return jnp.where(core == 0, i < self.half, i >= self.half)
        return i < self.half

    def send(self, i, core):
        half = self.half
        if self.descending:
            return jnp.where(core == 0, jnp.maximum(half - 1 - i, 0), jnp.minimum(half - 1, 2 * half - 1 - i))
        return jnp.minimum(i, half - 1)

    def keep(self, i, core):
        half = self.half
        if self.descending:
            return self.send(i, 1 - core)
        return jnp.maximum(i - half, 0)


def order_specs(order):
    row = lambda n: pl.BlockSpec((BLK, n), lambda i, c, *s: (order.block(i, c[0]), 0))
    local = lambda n: pl.BlockSpec((BLK, n), lambda i, c, *s: (order.local(i, c[0]), 0))
    send = lambda n: pl.BlockSpec((BLK, n), lambda i, c, *s: (order.send(i, c[0]), 0))
    keep = lambda n: pl.BlockSpec((BLK, n), lambda i, c, *s: (order.keep(i, c[0]), 0))
    return row, local, send, keep


def put(is_send, send_ref, keep_ref, value):
    @pl.when(is_send)
    def _():
        send_ref[...] = value

    @pl.when(jnp.logical_not(is_send))
    def _():
        keep_ref[...] = value


def attn_kernel(order, n_prev, core_ref, lo_ref, q_ref, k_ref, vt_ref, start_ref, wo_ref, *rest):
    rest = rest[n_prev:]
    o_ref, lse_ref, send_ref, keep_ref, acc_ref = rest
    i = pl.program_id(0)
    core = core_ref[0]
    block = order.block(i, core)
    start = start_ref[0]
    key_place = lax.broadcasted_iota(jnp.int32, (BLK, 2 * BLK), 0)
    acc_ref[...] = jnp.zeros_like(acc_ref)

    def step(kb, diagonal):
        at = pl.multiple_of(kb * BLK, BLK)
        keys = k_ref[pl.ds(at, BLK), :]
        allowed = key_place >= start - at
        if diagonal:
            lane = lax.broadcasted_iota(jnp.int32, (BLK, 2 * BLK), 1)
            allowed = allowed & (key_place <= lax.rem(lane, BLK))
        for group in range(2):
            scores = dot_nt(keys, q_ref[0, group]) * EXP2_SCALE
            probs = jnp.exp2(jnp.where(allowed, scores, BIG_NEGATIVE)).astype(BF16)
            acc_ref[group] += dot(vt_ref[group, :, pl.ds(at, BLK)], probs)

    def loop_body(kb, carry):
        step(kb, False)
        return carry

    lax.fori_loop(lo_ref[block], block, loop_body, 0)
    step(block, True)
    parts = []
    for group in range(2):
        total = acc_ref[group, HD:HD + 1, :]
        lse_ref[0, group:group + 1, :] = jnp.log2(total)
        heads = acc_ref[group, 0:HD, :] / total
        parts += [heads[:, :BLK], heads[:, BLK:]]
    out = jnp.concatenate(parts, axis=0).T.astype(BF16)
    o_ref[...] = out
    put(order.is_send(i, core), send_ref, keep_ref, dot_nt(out, wo_ref[...]).astype(BF16))


def attn_call(chunk, half, core, lo, q, k, vt, start, w, previous):
    seq = k.shape[0]
    width = w.shape[0]
    blocks = seq // BLK
    order = Order(chunk, half, False)
    row, _, send, keep = order_specs(order)
    n_prev = len(previous)
    by_block = lambda *tail: pl.BlockSpec((1,) + tail, lambda i, c, *s: (order.block(i, c[0]),) + (0,) * len(tail))
    return pl.pallas_call(
        functools.partial(attn_kernel, order, n_prev),
        grid_spec=pltpu.PrefetchScalarGridSpec(
            num_scalar_prefetch=2,
            grid=(2 * half,),
            in_specs=[
                by_block(2, 2 * BLK, 128), whole((seq, 128)), whole((2, HD + 16, seq)),
                by_block(1, 2 * BLK),
                pl.BlockSpec((width, 256), lambda i, *s: (0, 2)),
            ] + [ANY] * n_prev,
            out_specs=[row(256), by_block(2, 2 * BLK), send(width), keep(width)],
            scratch_shapes=[pltpu.VMEM((2, HD + 16, 2 * BLK), F32)],
        ),
        out_shape=[
            sds((seq, 256), BF16), sds((blocks, 2, 2 * BLK), F32),
            sds((half * BLK, width), BF16), sds((half * BLK, width), BF16),
        ],
        input_output_aliases={7 + j: j for j in range(n_prev)},
        compiler_params=params(),
        cost_estimate=cost(0.2 * 2 * half),
        name=f"attn_{chunk}",
    )(core, lo, q, k, vt, start, w, *previous)


def ffn_kernel(order, n_prev, hidden, core_ref, x_ref, own_ref, got_ref, g_ref, gain_ref, w_ref, *rest):
    rest = rest[n_prev:]
    xn_ref, dgu_ref, hid_ref, dsend_ref, dkeep_ref, ysend_ref, ykeep_ref = rest
    i = pl.program_id(0)
    is_send = order.is_send(i, core_ref[0])
    total = jnp.where(is_send, got_ref[...].astype(F32), own_ref[...].astype(F32))
    h = x_ref[...].astype(F32) + total
    rstd = lax.rsqrt(jnp.mean(h * h, axis=1, keepdims=True) + EPSILON)
    xn = (h * rstd * gain_ref[...]).astype(BF16)
    xn_ref[...] = xn
    gate_up = dot(xn, w_ref[:, :2 * hidden])
    gate, up = gate_up[:, :hidden], gate_up[:, hidden:]
    dhid = dot(g_ref[...], w_ref[:, 2 * hidden:])
    sig = 1.0 / (1.0 + jnp.exp(-gate))
    act = gate * sig
    hid = (act * up).astype(BF16)
    hid_ref[...] = hid
    dgate = (dhid * up * (sig * (1.0 + gate * (1.0 - sig)))).astype(BF16)
    dup = (dhid * act).astype(BF16)
    dgu_ref[:, :hidden] = dgate
    dgu_ref[:, hidden:] = dup
    dxn = dot_nt(dgu_ref[...], w_ref[:, :2 * hidden])
    put(is_send, dsend_ref, dkeep_ref, dxn.astype(BF16))
    put(is_send, ysend_ref, ykeep_ref, dot_nt(hid, w_ref[:, 2 * hidden:]).astype(BF16))


def ffn_call(chunk, half, core, x, own, got, g, gain, w, previous, y_previous):
    seq, width = x.shape
    hidden = w.shape[1] // 3
    order = Order(chunk, half, False)
    row, _, send, keep = order_specs(order)
    n_prev = len(previous) + len(y_previous)
    rows = half * BLK
    y_at = (chunk % 2) * half
    y_send = pl.BlockSpec((BLK, width), lambda i, c, *s: (y_at + order.send(i, c[0]), 0))
    y_keep = pl.BlockSpec((BLK, width), lambda i, c, *s: (y_at + order.keep(i, c[0]), 0))
    aliases = {7 + j: j for j in range(len(previous))}
    aliases.update({7 + len(previous) + j: 5 + j for j in range(len(y_previous))})
    return pl.pallas_call(
        functools.partial(ffn_kernel, order, n_prev, hidden),
        grid_spec=pltpu.PrefetchScalarGridSpec(
            num_scalar_prefetch=1,
            grid=(2 * half,),
            in_specs=[
                row(width), keep(width), send(width), row(width), whole((1, width)),
                pl.BlockSpec((width, 3 * hidden), lambda i, *s: (0, 0), pipeline_mode=pl.Buffered(1)),
            ] + [ANY] * n_prev,
            out_specs=[row(width), row(2 * hidden), row(hidden), send(width), keep(width), y_send, y_keep],
        ),
        out_shape=[sds((seq, width), BF16), sds((seq, 2 * hidden), BF16), sds((seq, hidden), BF16)]
        + [sds((rows, width), BF16)] * 2 + [sds((2 * rows, width), BF16)] * 2,
        input_output_aliases=aliases,
        compiler_params=params(),
        cost_estimate=cost(5 * 7.5 * 2 * half),
        name=f"ffn_{chunk}",
    )(core, x, own, got, g, gain, w, *previous, *y_previous)


def back_kernel(
    order, n_prev, first, core_ref, lo_ref, x_ref, own_ref, got_ref, down_ref, dgot_ref, g_ref, gain_ref,
    q_ref, k_ref, v_ref, kt_ref, o_ref, lse_ref, start_ref, wo_ref, wqkv_ref, z_ref, cos_ref, sin_ref,
    qgain_ref, kgain_ref, *rest,
):
    carried = () if first else rest[:2]
    rest = rest[n_prev + (0 if first else 2):]
    (dkv_k_ref, dkv_v_ref, dhb_ref, dz_ref, dh_ref, send_ref, keep_ref, fgain_ref, again_ref, hgain_ref,
     do_ref, dq_ref, delta_ref) = rest
    i = pl.program_id(0)
    core = core_ref[0]
    block = order.block(i, core)
    is_send = order.is_send(i, core)

    @pl.when(i == 0)
    def _():
        fgain_ref[...] = jnp.zeros_like(fgain_ref)
        again_ref[...] = jnp.zeros_like(again_ref)
        hgain_ref[...] = jnp.zeros_like(hgain_ref)
        if first:
            dkv_k_ref[...] = jnp.zeros_like(dkv_k_ref)
            dkv_v_ref[...] = jnp.zeros_like(dkv_v_ref)
        else:
            dkv_k_ref[...] = carried[0][...]
            dkv_v_ref[...] = carried[1][...]

    total = jnp.where(is_send, got_ref[...].astype(F32), own_ref[...].astype(F32))
    dxn = jnp.where(is_send, dgot_ref[...].astype(F32), down_ref[...].astype(F32))
    h = x_ref[...].astype(F32) + total
    rstd = lax.rsqrt(jnp.mean(h * h, axis=1, keepdims=True) + EPSILON)
    hhat = h * rstd
    fgain_ref[...] += jnp.sum(dxn * hhat, axis=0, keepdims=True)
    u = dxn * gain_ref[...]
    dh = g_ref[...].astype(F32) + rstd * (u - hhat * jnp.mean(u * hhat, axis=1, keepdims=True))
    dh_ref[...] = dh
    dhb = dh.astype(BF16)
    dhb_ref[...] = dhb
    dheads = dot(dhb, wo_ref[...]).astype(BF16).astype(F32)
    delta_t = (dheads * o_ref[...].astype(F32)).T
    for group in range(2):
        do_ref[group] = head_pads(dheads[:, group * 128:(group + 1) * 128], group)
        sums = [
            jnp.sum(delta_t[(2 * group + r) * HD:(2 * group + r + 1) * HD], axis=0, keepdims=True)
            for r in range(2)
        ]
        delta_ref[group:group + 1, :] = jnp.concatenate(sums, axis=1)
    dq_ref[...] = jnp.zeros_like(dq_ref)
    start = start_ref[0]
    key_place = lax.broadcasted_iota(jnp.int32, (BLK, 2 * BLK), 0)

    def step(kb, diagonal):
        at = pl.multiple_of(kb * BLK, BLK)
        keys = k_ref[pl.ds(at, BLK), :]
        values = v_ref[pl.ds(at, BLK), :]
        allowed = key_place >= start - at
        if diagonal:
            lane = lax.broadcasted_iota(jnp.int32, (BLK, 2 * BLK), 1)
            allowed = allowed & (key_place <= lax.rem(lane, BLK))
        dk = dkv_k_ref[pl.ds(at, BLK), :]
        dv = dkv_v_ref[pl.ds(at, BLK), :]
        for group in range(2):
            queries, douts = q_ref[0, group], do_ref[group]
            scores = dot_nt(keys, queries) * EXP2_SCALE - lse_ref[0, group:group + 1, :]
            probs = jnp.exp2(jnp.where(allowed, scores, BIG_NEGATIVE))
            dprobs = dot_nt(values, douts)
            dscores = (probs * (dprobs - delta_ref[group:group + 1, :])).astype(BF16)
            dv += dot(probs.astype(BF16), douts)
            dk += dot(dscores, queries)
            dq_ref[group] += dot(kt_ref[group * HD:(group + 1) * HD, pl.ds(at, BLK)], dscores)
        dkv_k_ref[pl.ds(at, BLK), :] = dk
        dkv_v_ref[pl.ds(at, BLK), :] = dv

    def loop_body(kb, carry):
        step(kb, False)
        return carry

    lax.fori_loop(lo_ref[block], block, loop_body, 0)
    step(block, True)

    parts = []
    for group in range(2):
        dq_t = dq_ref[group]
        parts += [dq_t[:, :BLK], dq_t[:, BLK:]]
    dq = jnp.concatenate(parts, axis=0).T * SCALE
    cos, sin = cos_ref[...], sin_ref[...]

    def post_back(grad, raw, gain):
        dn = grad * cos - swap_halves(grad) * sin
        rstd = lax.rsqrt(pair_mean(raw * raw) + EPSILON)
        hat = raw * rstd
        gain_grad = jnp.sum(dn * hat, axis=0, keepdims=True)
        dhat = dn * gain
        return rstd * (dhat - hat * pair_mean(dhat * hat)), gain_grad

    at = pl.multiple_of(block * BLK, BLK)
    qg = jnp.zeros((1, 128), F32)
    for group in range(2):
        lanes = slice(group * 128, (group + 1) * 128)
        dzq, gain_grad = post_back(dq[:, lanes], z_ref[:, lanes], qgain_ref[...])
        dz_ref[:, lanes] = dzq.astype(BF16)
        qg += gain_grad
    dzk, kg = post_back(dkv_k_ref[pl.ds(at, BLK), :] * SCALE, z_ref[:, 256:384], kgain_ref[...])
    dz_ref[:, 256:384] = dzk.astype(BF16)
    dz_ref[:, 384:512] = dkv_v_ref[pl.ds(at, BLK), :].astype(BF16)
    hgain_ref[0:1, :] += qg
    hgain_ref[1:2, :] += kg
    dxn_one = dot_nt(dz_ref[...], wqkv_ref[...]).astype(BF16)
    put(is_send, send_ref, keep_ref, dxn_one)
    x = x_ref[...].astype(F32)
    xhat = x * lax.rsqrt(jnp.mean(x * x, axis=1, keepdims=True) + EPSILON)
    again_ref[...] += jnp.sum(dxn_one.astype(F32) * xhat, axis=0, keepdims=True)


def back_call(chunk, half, core, lo, x, own, got, down, dgot, g, gain, q, k, v, kt, o, lse, start, w,
              z, cos, sin, qgain, kgain, carried, previous):
    seq, width = x.shape
    order = Order(chunk, half, True)
    row, local, send, keep = order_specs(order)
    first = len(previous) == 0
    n_prev = len(previous)
    rows = half * BLK
    by_block = lambda *tail: pl.BlockSpec((1,) + tail, lambda i, c, *s: (order.block(i, c[0]),) + (0,) * len(tail))
    n_in = 2 + 21
    extra = [] if first else [whole((seq, 128))] * 2 + [ANY] * n_prev
    return pl.pallas_call(
        functools.partial(back_kernel, order, n_prev, first),
        grid_spec=pltpu.PrefetchScalarGridSpec(
            num_scalar_prefetch=2,
            grid=(2 * half,),
            in_specs=[
                row(width), keep(width), send(width), keep(width), send(width), row(width), whole((1, width)),
                by_block(2, 2 * BLK, 128), whole((seq, 128)), whole((seq, 128)), whole((128, seq)),
                row(256), by_block(2, 2 * BLK), by_block(1, 2 * BLK),
                pl.BlockSpec((width, 256), lambda i, *s: (0, 2)),
                pl.BlockSpec((width, 512), lambda i, *s: (0, 0)),
                row(384), row(128), row(128), whole((1, 128)), whole((1, 128)),
            ] + extra,
            out_specs=[
                whole((seq, 128)), whole((seq, 128)), row(width), row(512), local(width),
                send(width), keep(width), whole((1, width)), whole((1, width)), whole((2, 128)),
            ],
            scratch_shapes=[
                pltpu.VMEM((2, 2 * BLK, 128), BF16),
                pltpu.VMEM((2, HD, 2 * BLK), F32),
                pltpu.VMEM((2, 2 * BLK), F32),
            ],
        ),
        out_shape=[
            sds((seq, 128), F32), sds((seq, 128), F32), sds((seq, width), BF16), sds((seq, 512), BF16),
            sds((2 * rows, width), F32), sds((rows, width), BF16), sds((rows, width), BF16),
            sds((1, width), F32), sds((1, width), F32), sds((2, 128), F32),
        ],
        input_output_aliases={n_in + 2 + j: 2 + j for j in range(n_prev)},
        compiler_params=params(),
        cost_estimate=cost(5 * 7.5 * 2 * half),
        name=f"back_{chunk}",
    )(core, lo, x, own, got, down, dgot, g, gain, q, k, v, kt, o, lse, start, w, w, z, cos, sin,
      qgain, kgain, *carried, *previous)


def input_kernel(order, n_prev, core_ref, dh_ref, x_ref, own_ref, got_ref, gain_ref, *rest):
    (out_ref,) = rest[n_prev:]
    i = pl.program_id(0)
    is_send = order.is_send(i, core_ref[0])
    dxn = jnp.where(is_send, got_ref[...].astype(F32), own_ref[...].astype(F32))
    x = x_ref[...].astype(F32)
    rstd = lax.rsqrt(jnp.mean(x * x, axis=1, keepdims=True) + EPSILON)
    xhat = x * rstd
    u = dxn * gain_ref[...]
    out_ref[...] = dh_ref[...] + rstd * (u - xhat * jnp.mean(u * xhat, axis=1, keepdims=True))


def input_call(chunk, half, core, dh, x, own, got, gain, previous):
    seq, width = x.shape
    order = Order(chunk, half, False)
    row, local, send, keep = order_specs(order)
    n_prev = len(previous)
    return pl.pallas_call(
        functools.partial(input_kernel, order, n_prev),
        grid_spec=pltpu.PrefetchScalarGridSpec(
            num_scalar_prefetch=1,
            grid=(2 * half,),
            in_specs=[local(width), row(width), keep(width), send(width), whole((1, width))] + [ANY] * n_prev,
            out_specs=[row(width)],
        ),
        out_shape=[sds((seq, width), F32)],
        input_output_aliases={6 + j: j for j in range(n_prev)},
        compiler_params=params(),
        cost_estimate=cost(5 * 2 * 2 * half),
        name=f"grad_input_{chunk}",
    )(core, dh, x, own, got, gain, *previous)


def output_kernel(core_ref, x_ref, *refs):
    (out_ref,) = refs[-1:]
    chunk = pl.program_id(0)
    mine = pl.program_id(1) == core_ref[0]
    for index in range(CHUNKS):
        own_ref, got_ref = refs[2 * index:2 * index + 2]
        yown_ref, ygot_ref = refs[2 * CHUNKS + 2 * (index // 2):2 * CHUNKS + 2 * (index // 2) + 2]
        for kept in range(2):
            @pl.when((chunk == index) & (mine if kept else jnp.logical_not(mine)))
            def _(a_ref=own_ref if kept else got_ref, y_ref=yown_ref if kept else ygot_ref):
                total = a_ref[...].astype(F32) + y_ref[...].astype(F32)
                out_ref[...] = (x_ref[...].astype(F32) + total).astype(BF16)


def output_call(half, core, x, attn_sums, y_sums):
    seq, width = x.shape
    rows = BLK
    per = half * BLK // rows
    row = pl.BlockSpec((rows, width), lambda c, h, i, *s: ((c * 2 + h) * per + i, 0))

    def moving(index):
        def at(c, h, i, *s):
            return (jnp.where(c == index, i, jnp.where(c < index, 0, per - 1)), 0)

        return pl.BlockSpec((rows, width), at)

    def y_moving(pair):
        def at(c, h, i, *s):
            here = lax.rem(c, 2) * per + i
            return (jnp.where(c // 2 == pair, here, jnp.where(c // 2 < pair, 0, 2 * per - 1)), 0)

        return pl.BlockSpec((rows, width), at)

    args, specs = [], []
    for index in range(CHUNKS):
        args += list(attn_sums[index])
        specs += [moving(index)] * 2
    for pair in range(CHUNKS // 2):
        args += list(y_sums[pair])
        specs += [y_moving(pair)] * 2
    return pl.pallas_call(
        output_kernel,
        grid_spec=pltpu.PrefetchScalarGridSpec(
            num_scalar_prefetch=1,
            grid=(CHUNKS, 2, per),
            in_specs=[row] + specs,
            out_specs=row,
        ),
        out_shape=sds((seq, width), BF16),
        compiler_params=pltpu.CompilerParams(
            dimension_semantics=("arbitrary",) * 3, vmem_limit_bytes=56 * 1024 * 1024
        ),
        cost_estimate=cost(5 * 8),
        name="output",
    )(core, x, *args)


def pack_kernel(wq_ref, wk_ref, wv_ref, wo_ref, gain_ref, wg_ref, wu_ref, wd_ref, attn_ref, ffn_ref):
    queries, keys = wq_ref.shape[1], wk_ref.shape[1]
    hidden = wg_ref.shape[1]
    attn_ref[:, :queries] = wq_ref[...]
    attn_ref[:, queries:queries + keys] = wk_ref[...]
    attn_ref[:, queries + keys:queries + 2 * keys] = wv_ref[...]
    at = queries + 2 * keys
    attn_ref[:, at:at + queries] = wo_ref[...].astype(F32).T.astype(BF16)
    attn_ref[:, at + queries:] = gain_ref[...].astype(F32).T.astype(BF16)
    ffn_ref[:, :hidden] = wg_ref[...]
    ffn_ref[:, hidden:2 * hidden] = wu_ref[...]
    ffn_ref[:, 2 * hidden:] = wd_ref[...].astype(F32).T.astype(BF16)


def pack(w_query, w_key, w_value, w_out, attn_gain, ffn_gain, w_gate, w_up, w_down):
    shard = w_query.shape[0]
    if shard % 128:
        gains = jnp.stack([attn_gain, ffn_gain] + [jnp.zeros_like(attn_gain)] * 126, axis=1)
        return (
            jnp.concatenate([w_query, w_key, w_value, w_out.T, gains], axis=1),
            jnp.concatenate([w_gate, w_up, w_down.T], axis=1),
        )
    gains = jnp.concatenate([attn_gain[None], ffn_gain[None], jnp.zeros((126, shard), BF16)], axis=0)
    columns = 2 * w_query.shape[1] + 2 * w_key.shape[1] + 128
    return pl.pallas_call(
        pack_kernel,
        out_shape=[sds((shard, columns), BF16), sds((shard, 3 * w_gate.shape[1]), BF16)],
        cost_estimate=cost(3),
        name="pack",
    )(w_query, w_key, w_value, w_out, gains, w_gate, w_up, w_down)


def dp_place(n_dp):
    at = lax.axis_index("dp")
    return at // 2, lax.rem(at, 2)


def ring_of(n_dp):
    return [(i, (i + 2) % n_dp) for i in range(n_dp)]


PAIR = [(i, i ^ 1) for i in range(8)]


def place_kernel(at_ref, *refs):
    pieces, out_ref = refs[:8], refs[8]
    i = pl.program_id(0)
    step = lax.rem(at_ref[0] + 4 - i // 2, 4)
    same = lax.rem(i, 2) == at_ref[1]
    for index in range(4):
        for own in range(2):
            @pl.when((step == index) & (same if own else jnp.logical_not(same)))
            def _(ref=pieces[index + 4 * (1 - own)]):
                out_ref[...] = ref[...]


def place_pieces(line, other, z, y):
    rows, columns = line[0].shape
    return pl.pallas_call(
        place_kernel,
        grid_spec=pltpu.PrefetchScalarGridSpec(
            num_scalar_prefetch=1,
            grid=(8,),
            in_specs=[
                pl.BlockSpec((rows, columns), lambda i, *s: (0, 0), pipeline_mode=pl.Buffered(1))
            ] * 8,
            out_specs=pl.BlockSpec((rows, columns), lambda i, *s: (i, 0)),
        ),
        out_shape=sds((8 * rows, columns), line[0].dtype),
        compiler_params=params(),
        cost_estimate=cost(0.2),
        name="place_pieces",
    )(jnp.stack([z, y]).astype(jnp.int32), *line, *other)


class Gather:
    def __init__(self, piece, n_dp, *clear):
        self.n_dp, self.piece, self.line, self.other = n_dp, piece, [], []
        if n_dp == 8:
            self.step(piece, *clear)

    def step(self, piece, *clear):
        self.line.append(piece)
        self.other.append(lax.ppermute(after(piece, *clear) if clear else piece, "dp", PAIR))

    def relay(self, *ahead):
        if self.n_dp == 8:
            piece = self.line[-1]
            if len(self.line) > 1:
                piece = after(piece, self.other[-2])
            piece = lax.ppermute(piece, "dp", ring_of(8))
            self.step(after(piece, *ahead) if ahead else piece)
            return self.line[-1]
        return self.piece

    def crossed(self, at):
        return self.other[at] if self.n_dp == 8 else self.piece

    def result(self, turn=None):
        if self.n_dp != 8:
            return lax.all_gather(self.piece, "dp", axis=0, tiled=True)
        z, y = dp_place(8)
        if turn is not None:
            z = after(z, turn)
        return place_pieces(self.line, self.other, z, y)


class Lane:
    def __init__(self, steps):
        self.steps, self.waits = steps, None
        self.move(None)

    def move(self, values):
        try:
            self.waits = self.steps.send(values)
        except StopIteration:
            self.waits = None


def advance(token, lanes, *extra):
    lanes = [lane for lane in lanes if lane.waits is not None]
    values, token, _ = lax.optimization_barrier(([lane.waits for lane in lanes], token, extra))
    for lane, value in zip(lanes, values):
        lane.move(value)
    return token


def scatter(grad, n_dp, store, key, crossings):
    if n_dp != 8:
        store[key] = lax.psum_scatter(grad, "dp", scatter_dimension=0, tiled=True).astype(F32)
        crossings += [grad] * 2
        return
    z, y = dp_place(n_dp)
    rows, columns = grad.shape[0] // n_dp, grad.shape[1]

    def part(step, line):
        at = (lax.rem(z + 4 - step, 4) * 2 + line) * rows
        return lax.dynamic_slice(grad, (at, 0), (rows, columns))

    kept = [part(step, y) for step in (1, 2, 3, 4)]
    for step in (1, 3):
        parts = jnp.concatenate([part(step, 1 - y), part(step + 1, 1 - y)], axis=0)
        crossings.append(lax.ppermute(parts, "dp", PAIR))
    passed = ()
    for step in range(4):
        crossed, *values = yield (crossings[step // 2],) + passed
        total = kept[step].astype(F32)
        for value in [crossed[step % 2 * rows:(step % 2 + 1) * rows]] + values:
            total = total + value.astype(F32)
        if step < 3:
            passed = (lax.ppermute(total.astype(BF16), "dp", ring_of(8)),)
    store[key] = total


NEAR = [(t, t ^ 1) for t in range(4)]
FAR = [(t, t ^ 2) for t in range(4)]


def sum_tensor(send, keep, store, key):
    (got,) = yield (lax.ppermute(send, "tensor", NEAR),)
    mine = (keep.astype(F32) + got.astype(F32)).astype(BF16)
    (got,) = yield (lax.ppermute(mine, "tensor", FAR),)
    own = (mine.astype(F32) + got.astype(F32)).astype(BF16)
    (got,) = yield (lax.ppermute(own, "tensor", NEAR),)
    store[key] = (own, got)


def sum_all(value, n_dp, store, key):
    for axis, size in (("tensor", 4), ("dp", n_dp)):
        bit = 1
        while bit < size:
            (got,) = yield (lax.ppermute(value, axis, [(i, i ^ bit) for i in range(size)]),)
            value = value + got
            bit *= 2
    store[key] = value


def body(
    tokens, segment_ids, positions, pad_mask, w_query, w_key, w_value, w_out, w_gate, w_up, w_down,
    attn_gain, ffn_gain, query_gain, key_gain, cotangent,
):
    del segment_ids
    seq, width = tokens.shape
    shard = w_query.shape[0]
    n_dp = width // shard
    hidden = w_gate.shape[1]
    chunks = CHUNKS
    half = seq // chunks // 2 // BLK
    blocks = seq // BLK
    core_id = lax.rem(lax.axis_index("tensor"), 2).astype(jnp.int32).reshape(1)

    place = jnp.arange(seq, dtype=jnp.int32)
    start = jnp.where(pad_mask == 1, place - positions, place)
    lo = (place[::BLK] - positions[::BLK]) // BLK
    start_rows = jnp.tile(start.reshape(blocks, 1, BLK), (1, 1, 2))
    half_size = HD // 2
    inverse = THETA ** (-(jnp.arange(half_size).astype(F32) * 2.0 / HD))
    angles = positions.astype(F32)[:, None] * inverse[None, :]
    cos_half, sin_half = jnp.cos(angles), jnp.sin(angles)
    cos = jnp.concatenate([cos_half] * 4, axis=1)
    sin = jnp.concatenate([-sin_half, sin_half] * 2, axis=1)

    attn_piece, ffn_piece = pack(
        w_query, w_key, w_value, w_out, attn_gain, ffn_gain, w_gate, w_up, w_down
    )
    gather_attn = Gather(attn_piece, n_dp)
    gather_attn.relay()
    gather_attn.relay(cos, sin)
    late = gather_attn.relay()
    w_attn = gather_attn.result()
    gather_ffn = Gather(after(ffn_piece, late), n_dp, *gather_attn.other)
    gain_rows = w_attn[:, 768:770].T.astype(F32)
    attn_scales, ffn_scales = gain_rows[0:1], gain_rows[1:2]
    query_scales = jnp.tile(query_gain.astype(F32), 2)[None]
    key_scales = jnp.tile(key_gain.astype(F32), 2)[None]

    line_one = gather_ffn.relay(w_attn)
    xn_one, z, q, k, v, kt, vt = qkv_call(
        tokens, attn_scales, w_attn, cos, sin, query_scales, key_scales
    )
    order = list(range(chunks))[::-1]
    previous = ()
    attn_sum, ffn_grad_sum, y_sums, input_grad_sum, dhs, totals = {}, {}, {}, {}, {}, {}
    lanes = []
    for step, c in enumerate(order):
        turn = core_id
        if step == 0:
            turn = after(turn, line_one, gather_ffn.crossed(0))
            line_two = gather_ffn.relay()
        if step == 1:
            turn = after(turn, line_two, gather_ffn.crossed(1))
            line_three = gather_ffn.relay()
        if step == 2:
            turn = advance(turn, [lanes[0]])
        if step == 3:
            turn = advance(turn, [lanes[1]])
        heads, lse, send, keep = attn_call(c, half, turn, lo, q, k, vt, start_rows, w_attn, previous)
        previous = (heads, lse)
        lanes.append(Lane(sum_tensor(send, keep, attn_sum, c)))
    turn = advance(core_id, [lanes[0], lanes[2], lanes[3]], line_three, gather_ffn.crossed(2))
    turn = advance(turn, [lanes[0], lanes[1]], gather_ffn.crossed(3))
    w_ffn = gather_ffn.result(turn)
    late = lanes
    previous, y_previous = (), ()
    lanes, y_lanes = [], []
    for step, c in enumerate(order):
        if step == 1:
            turn = advance(after(core_id, dsend), late[1:3])
        if step == 2:
            turn = advance(after(core_id, dsend), late[2:4] + [lanes[0]])
        if step == 3:
            turn = advance(after(core_id, dsend), [late[3], lanes[0], lanes[1]])
        own, got = attn_sum[c]
        xn_two, dgu, hid, dsend, dkeep, ysend, ykeep = ffn_call(
            c, half, turn, tokens, own, got, cotangent, ffn_scales, w_ffn, previous, y_previous
        )
        previous = (xn_two, dgu, hid)
        y_previous = (ysend, ykeep) if c % 2 else ()
        lanes.append(Lane(sum_tensor(dsend, dkeep, ffn_grad_sum, c)))
        if c % 2 == 0:
            y_lanes.append(Lane(sum_tensor(ysend, ykeep, y_sums, c // 2)))
    tn = (((0,), (0,)), ((), ()))
    turn = advance(after(core_id, dsend), lanes[:3])
    hid = after(hid, turn)
    grad_down_t = lax.dot_general(cotangent, hid, tn, preferred_element_type=F32).astype(BF16)
    down_got, gate_up_got, attn_got = [], [], []
    down_lane = Lane(scatter(grad_down_t, n_dp, totals, "down", down_got))
    turn = advance(after(core_id, grad_down_t), lanes[1:4])
    dgu = after(dgu, turn)
    grad_gate_up = lax.dot_general(xn_two, dgu, tn, preferred_element_type=F32).astype(BF16)
    gate_up_lane = Lane(scatter(grad_gate_up, n_dp, totals, "gate_up", gate_up_got))

    previous, carried = (), ()
    ffn_gain_grad = jnp.zeros((1, width), F32)
    attn_gain_grad = jnp.zeros((1, width), F32)
    head_gain_grad = jnp.zeros((2, 128), F32)
    back_lanes = []
    for step, c in enumerate(order):
        if step == 0:
            turn = advance(
                after(core_id, grad_gate_up), [lanes[2], y_lanes[0], down_lane], *down_got[:1]
            )
        if step == 1:
            turn = advance(after(core_id, hg), [lanes[3], y_lanes[1], down_lane], *down_got)
        if step == 2:
            turn = advance(
                after(core_id, hg), [lanes[3], y_lanes[0], back_lanes[0], down_lane, gate_up_lane]
            )
        if step == 3:
            turn = advance(
                after(core_id, hg), y_lanes + [back_lanes[0], back_lanes[1], down_lane, gate_up_lane]
            )
        own, got = attn_sum[c]
        down, dgot = ffn_grad_sum[c]
        dk, dv, dhb, dz, dhs[c], send, keep, fg, ag, hg = back_call(
            c, half, turn, lo, tokens, own, got, down, dgot, cotangent, ffn_scales, q, k, v, kt,
            heads, lse, start_rows, w_attn, z, cos, sin, query_scales, key_scales, carried, previous,
        )
        carried, previous = (dk, dv), (dhb, dz)
        ffn_gain_grad += fg
        attn_gain_grad += ag
        head_gain_grad += hg
        back_lanes.append(Lane(sum_tensor(send, keep, input_grad_sum, c)))

    turn = advance(after(core_id, hg), back_lanes[:3] + [y_lanes[1], gate_up_lane])
    head_gains = head_gain_grad[:, :HD] + head_gain_grad[:, HD:]
    small = jnp.concatenate(
        [attn_gain_grad.reshape(-1), 0.25 * ffn_gain_grad.reshape(-1), head_gains.reshape(-1)]
    )
    small_lane = Lane(sum_all(small.reshape(-1, 128), n_dp, totals, "small"))
    dz = after(dz, turn)
    grad_qkv = lax.dot_general(xn_one, dz, tn, preferred_element_type=F32).astype(BF16)
    grad_out_t = lax.dot_general(dhb, heads, tn, preferred_element_type=F32).astype(BF16)
    grad_attn = jnp.concatenate([grad_qkv, grad_out_t], axis=1)
    attn_lane = Lane(scatter(grad_attn, n_dp, totals, "attn", attn_got))
    turn = advance(after(core_id, grad_attn), [back_lanes[3], small_lane])
    output = output_call(half, turn, tokens, attn_sum, y_sums)
    turn = advance(
        after(core_id, output), [attn_lane, back_lanes[1], back_lanes[2], small_lane, gate_up_lane], *attn_got
    )

    previous_in = ()
    for step, c in enumerate(order):
        if step == 2:
            turn = advance(after(core_id, grad_input), [attn_lane, back_lanes[2], back_lanes[3], small_lane])
        if step == 3:
            turn = advance(after(core_id, grad_input), [attn_lane, back_lanes[3], small_lane])
        eown, egot = input_grad_sum[c]
        (grad_input,) = input_call(c, half, turn, dhs[c], tokens, eown, egot, attn_scales, previous_in)
        previous_in = (grad_input,)
    while attn_lane.waits is not None or small_lane.waits is not None:
        turn = advance(turn, [attn_lane, small_lane])
    down_own, gate_up_own, attn_own = totals["down"], totals["gate_up"], totals["attn"]
    small = totals["small"].reshape(-1)
    mine = lax.axis_index("dp") * shard
    grad_attn_gain = lax.dynamic_slice(small, (mine,), (shard,))
    grad_ffn_gain = lax.dynamic_slice(small, (width + mine,), (shard,))
    return (
        output,
        grad_input,
        attn_own[:, :256],
        attn_own[:, 256:384],
        attn_own[:, 384:512],
        attn_own[:, 512:768].T,
        gate_up_own[:, :hidden],
        gate_up_own[:, hidden:],
        down_own.T,
        grad_attn_gain,
        grad_ffn_gain,
        small[2 * width:2 * width + HD],
        small[2 * width + HD:],
    )


def solution(mesh):
    rows, flat, both = P("dp", None), P("dp"), P("dp", "tensor")
    columns = P("tensor", "dp")
    return jax.shard_map(
        body,
        mesh=mesh,
        in_specs=(
            rows, flat, flat, flat, both, both, both, columns, both, both, columns, flat, flat, P(), P(), rows,
        ),
        out_specs=(rows, rows, both, both, both, columns, both, both, columns, flat, flat, P(), P()),
        check_vma=False,
    )
```

```python
import functools
import math

import jax
import jax.numpy as jnp
from jax import lax
from jax.experimental import pallas as pl
from jax.experimental.pallas import tpu as pltpu
from jax.sharding import PartitionSpec as P

HD = 64
EPSILON = 1e-05
THETA = 1000000.0
BIG_NEGATIVE = -1e30
CHUNKS = 4
BLK = 256
F32 = jnp.float32
BF16 = jnp.bfloat16
SCALE = 1.0 / math.sqrt(HD)
EXP2_SCALE = SCALE * math.log2(math.e)
NT = (((1,), (1,)), ((), ()))
ANY = pl.BlockSpec(memory_space=pl.ANY)


def sds(shape, dtype):
    return jax.ShapeDtypeStruct(shape, dtype)


def whole(shape):
    return pl.BlockSpec(shape, lambda i, *s: (0,) * len(shape))


def dot(left, right):
    return jnp.dot(left, right, preferred_element_type=F32)


def dot_nt(left, right):
    return lax.dot_general(left, right, NT, preferred_element_type=F32)


def cost(micros):
    return pl.CostEstimate(flops=0, bytes_accessed=int(micros * 3.4e6), transcendentals=0)


def after(value, *others):
    return lax.optimization_barrier((value, others))[0]


def params():
    return pltpu.CompilerParams(
        dimension_semantics=("arbitrary",), vmem_limit_bytes=56 * 1024 * 1024
    )


def low_half(shape, period):
    lane = lax.broadcasted_iota(jnp.int32, shape, 1)
    return lax.rem(lane, period) < period // 2


def swap_halves(values):
    left = pltpu.roll(values, 128 - HD // 2, 1)
    right = pltpu.roll(values, HD // 2, 1)
    return jnp.where(low_half(values.shape, HD), left, right)


def pair_mean(values):
    first = low_half(values.shape, 2 * HD)
    low = jnp.sum(jnp.where(first, values, 0.0), axis=1, keepdims=True)
    high = jnp.sum(jnp.where(first, 0.0, values), axis=1, keepdims=True)
    return jnp.where(first, low, high) * (1.0 / HD)


def head_pads(slab, group):
    first = low_half(slab.shape, 2 * HD)
    rolled = pltpu.roll(slab, HD, 1)
    if group == 0:
        pieces = (jnp.where(first, slab, 0.0), jnp.where(first, rolled, 0.0))
    else:
        pieces = (jnp.where(first, 0.0, rolled), jnp.where(first, 0.0, slab))
    return jnp.concatenate(pieces, axis=0).astype(BF16)


def qkv_kernel(
    x_ref, gain_ref, w_ref, cos_ref, sin_ref, qgain_ref, kgain_ref,
    xn_ref, z_ref, q_ref, k_ref, v_ref, kt_ref, vt_ref,
):
    x = x_ref[...].astype(F32)
    rstd = lax.rsqrt(jnp.mean(x * x, axis=1, keepdims=True) + EPSILON)
    xn = (x * rstd * gain_ref[...]).astype(BF16)
    xn_ref[...] = xn
    z = dot(xn, w_ref[...])
    z_ref[...] = z[:, :384]
    cos, sin = cos_ref[...], sin_ref[...]

    def post(values, gain):
        normed = values * lax.rsqrt(pair_mean(values * values) + EPSILON) * gain
        return normed * cos + swap_halves(normed) * sin

    for group in range(2):
        slab = post(z[:, group * 128:(group + 1) * 128], qgain_ref[...])
        q_ref[0, group] = head_pads(slab, group)
    keys = post(z[:, 256:384], kgain_ref[...])
    k_ref[...] = keys.astype(BF16)
    kt_ref[...] = keys.T.astype(BF16)
    values = z[:, 384:512]
    v_ref[...] = values.astype(BF16)
    values_t = values.T.astype(BF16)
    rows = lax.broadcasted_iota(jnp.int32, (16, BLK), 0)
    ones = jnp.where(rows == 0, 1.0, 0.0).astype(BF16)
    for group in range(2):
        vt_ref[group, 0:HD, :] = values_t[group * HD:(group + 1) * HD]
        vt_ref[group, HD:HD + 16, :] = ones


def qkv_call(x, gain, w, cos, sin, qgain, kgain):
    seq, width = x.shape
    blocks = seq // BLK
    row = lambda n: pl.BlockSpec((BLK, n), lambda i: (i, 0))
    return pl.pallas_call(
        qkv_kernel,
        grid=(blocks,),
        in_specs=[
            row(width), whole((1, width)), pl.BlockSpec((width, 512), lambda i: (0, 0)),
            row(128), row(128), whole((1, 128)), whole((1, 128)),
        ],
        out_specs=[
            row(width), row(384),
            pl.BlockSpec((1, 2, 2 * BLK, 128), lambda i: (i, 0, 0, 0)),
            row(128), row(128),
            pl.BlockSpec((128, BLK), lambda i: (0, i)),
            pl.BlockSpec((2, HD + 16, BLK), lambda i: (0, 0, i)),
        ],
        out_shape=[
            sds((seq, width), BF16), sds((seq, 384), F32),
            sds((blocks, 2, 2 * BLK, 128), BF16),
            sds((seq, 128), BF16), sds((seq, 128), BF16),
            sds((128, seq), BF16), sds((2, HD + 16, seq), BF16),
        ],
        compiler_params=params(),
        cost_estimate=cost(0.6),
        name="qkv",
    )(x, gain, w, cos, sin, qgain, kgain)


class Order:
    def __init__(self, chunk, half, descending):
        self.chunk, self.half, self.descending = chunk, half, descending

    def local(self, i, core):
        half = self.half
        if self.descending:
            return 2 * half - 1 - i
        first = i < half
        base = jnp.where(first, (1 - core) * half, core * half)
        return base + jnp.where(first, i, i - half)

    def block(self, i, core):
        return self.chunk * 2 * self.half + self.local(i, core)

    def is_send(self, i, core):
        if self.descending:
            return jnp.where(core == 0, i < self.half, i >= self.half)
        return i < self.half

    def send(self, i, core):
        half = self.half
        if self.descending:
            return jnp.where(core == 0, jnp.maximum(half - 1 - i, 0), jnp.minimum(half - 1, 2 * half - 1 - i))
        return jnp.minimum(i, half - 1)

    def keep(self, i, core):
        half = self.half
        if self.descending:
            return self.send(i, 1 - core)
        return jnp.maximum(i - half, 0)


def order_specs(order):
    row = lambda n: pl.BlockSpec((BLK, n), lambda i, c, *s: (order.block(i, c[0]), 0))
    local = lambda n: pl.BlockSpec((BLK, n), lambda i, c, *s: (order.local(i, c[0]), 0))
    send = lambda n: pl.BlockSpec((BLK, n), lambda i, c, *s: (order.send(i, c[0]), 0))
    keep = lambda n: pl.BlockSpec((BLK, n), lambda i, c, *s: (order.keep(i, c[0]), 0))
    return row, local, send, keep


def put(is_send, send_ref, keep_ref, value):
    @pl.when(is_send)
    def _():
        send_ref[...] = value

    @pl.when(jnp.logical_not(is_send))
    def _():
        keep_ref[...] = value


def attn_kernel(order, n_prev, core_ref, lo_ref, q_ref, k_ref, vt_ref, start_ref, wo_ref, *rest):
    rest = rest[n_prev:]
    o_ref, lse_ref, send_ref, keep_ref, acc_ref = rest
    i = pl.program_id(0)
    core = core_ref[0]
    block = order.block(i, core)
    start = start_ref[0]
    key_place = lax.broadcasted_iota(jnp.int32, (BLK, 2 * BLK), 0)
    acc_ref[...] = jnp.zeros_like(acc_ref)

    def step(kb, diagonal):
        at = pl.multiple_of(kb * BLK, BLK)
        keys = k_ref[pl.ds(at, BLK), :]
        allowed = key_place >= start - at
        if diagonal:
            lane = lax.broadcasted_iota(jnp.int32, (BLK, 2 * BLK), 1)
            allowed = allowed & (key_place <= lax.rem(lane, BLK))
        for group in range(2):
            scores = dot_nt(keys, q_ref[0, group]) * EXP2_SCALE
            probs = jnp.exp2(jnp.where(allowed, scores, BIG_NEGATIVE)).astype(BF16)
            acc_ref[group] += dot(vt_ref[group, :, pl.ds(at, BLK)], probs)

    def loop_body(kb, carry):
        step(kb, False)
        return carry

    lax.fori_loop(lo_ref[block], block, loop_body, 0)
    step(block, True)
    parts = []
    for group in range(2):
        total = acc_ref[group, HD:HD + 1, :]
        lse_ref[0, group:group + 1, :] = jnp.log2(total)
        heads = acc_ref[group, 0:HD, :] / total
        parts += [heads[:, :BLK], heads[:, BLK:]]
    out = jnp.concatenate(parts, axis=0).T.astype(BF16)
    o_ref[...] = out
    put(order.is_send(i, core), send_ref, keep_ref, dot_nt(out, wo_ref[...]).astype(BF16))


def attn_call(chunk, half, core, lo, q, k, vt, start, w, previous):
    seq = k.shape[0]
    width = w.shape[0]
    blocks = seq // BLK
    order = Order(chunk, half, False)
    row, _, send, keep = order_specs(order)
    n_prev = len(previous)
    by_block = lambda *tail: pl.BlockSpec((1,) + tail, lambda i, c, *s: (order.block(i, c[0]),) + (0,) * len(tail))
    return pl.pallas_call(
        functools.partial(attn_kernel, order, n_prev),
        grid_spec=pltpu.PrefetchScalarGridSpec(
            num_scalar_prefetch=2,
            grid=(2 * half,),
            in_specs=[
                by_block(2, 2 * BLK, 128), whole((seq, 128)), whole((2, HD + 16, seq)),
                by_block(1, 2 * BLK),
                pl.BlockSpec((width, 256), lambda i, *s: (0, 2)),
            ] + [ANY] * n_prev,
            out_specs=[row(256), by_block(2, 2 * BLK), send(width), keep(width)],
            scratch_shapes=[pltpu.VMEM((2, HD + 16, 2 * BLK), F32)],
        ),
        out_shape=[
            sds((seq, 256), BF16), sds((blocks, 2, 2 * BLK), F32),
            sds((half * BLK, width), BF16), sds((half * BLK, width), BF16),
        ],
        input_output_aliases={7 + j: j for j in range(n_prev)},
        compiler_params=params(),
        cost_estimate=cost(0.2 * 2 * half),
        name=f"attn_{chunk}",
    )(core, lo, q, k, vt, start, w, *previous)


def ffn_kernel(order, n_prev, hidden, core_ref, x_ref, own_ref, got_ref, g_ref, gain_ref, w_ref, *rest):
    rest = rest[n_prev:]
    xn_ref, dgu_ref, hid_ref, dsend_ref, dkeep_ref, ysend_ref, ykeep_ref = rest
    i = pl.program_id(0)
    is_send = order.is_send(i, core_ref[0])
    total = jnp.where(is_send, got_ref[...].astype(F32), own_ref[...].astype(F32))
    h = x_ref[...].astype(F32) + total
    rstd = lax.rsqrt(jnp.mean(h * h, axis=1, keepdims=True) + EPSILON)
    xn = (h * rstd * gain_ref[...]).astype(BF16)
    xn_ref[...] = xn
    gate_up = dot(xn, w_ref[:, :2 * hidden])
    gate, up = gate_up[:, :hidden], gate_up[:, hidden:]
    dhid = dot(g_ref[...], w_ref[:, 2 * hidden:])
    sig = 1.0 / (1.0 + jnp.exp(-gate))
    act = gate * sig
    hid = (act * up).astype(BF16)
    hid_ref[...] = hid
    dgate = (dhid * up * (sig * (1.0 + gate * (1.0 - sig)))).astype(BF16)
    dup = (dhid * act).astype(BF16)
    dgu_ref[:, :hidden] = dgate
    dgu_ref[:, hidden:] = dup
    dxn = dot_nt(dgu_ref[...], w_ref[:, :2 * hidden])
    put(is_send, dsend_ref, dkeep_ref, dxn.astype(BF16))
    put(is_send, ysend_ref, ykeep_ref, dot_nt(hid, w_ref[:, 2 * hidden:]).astype(BF16))


def ffn_call(chunk, half, core, x, own, got, g, gain, w, previous, y_previous):
    seq, width = x.shape
    hidden = w.shape[1] // 3
    order = Order(chunk, half, False)
    row, _, send, keep = order_specs(order)
    n_prev = len(previous) + len(y_previous)
    rows = half * BLK
    y_at = (chunk % 2) * half
    y_send = pl.BlockSpec((BLK, width), lambda i, c, *s: (y_at + order.send(i, c[0]), 0))
    y_keep = pl.BlockSpec((BLK, width), lambda i, c, *s: (y_at + order.keep(i, c[0]), 0))
    aliases = {7 + j: j for j in range(len(previous))}
    aliases.update({7 + len(previous) + j: 5 + j for j in range(len(y_previous))})
    return pl.pallas_call(
        functools.partial(ffn_kernel, order, n_prev, hidden),
        grid_spec=pltpu.PrefetchScalarGridSpec(
            num_scalar_prefetch=1,
            grid=(2 * half,),
            in_specs=[
                row(width), keep(width), send(width), row(width), whole((1, width)),
                pl.BlockSpec((width, 3 * hidden), lambda i, *s: (0, 0), pipeline_mode=pl.Buffered(1)),
            ] + [ANY] * n_prev,
            out_specs=[row(width), row(2 * hidden), row(hidden), send(width), keep(width), y_send, y_keep],
        ),
        out_shape=[sds((seq, width), BF16), sds((seq, 2 * hidden), BF16), sds((seq, hidden), BF16)]
        + [sds((rows, width), BF16)] * 2 + [sds((2 * rows, width), BF16)] * 2,
        input_output_aliases=aliases,
        compiler_params=params(),
        cost_estimate=cost(5 * 7.5 * 2 * half),
        name=f"ffn_{chunk}",
    )(core, x, own, got, g, gain, w, *previous, *y_previous)


def back_kernel(
    order, n_prev, first, core_ref, lo_ref, x_ref, own_ref, got_ref, down_ref, dgot_ref, g_ref, gain_ref,
    q_ref, k_ref, v_ref, kt_ref, o_ref, lse_ref, start_ref, wo_ref, wqkv_ref, z_ref, cos_ref, sin_ref,
    qgain_ref, kgain_ref, *rest,
):
    carried = () if first else rest[:2]
    rest = rest[n_prev + (0 if first else 2):]
    (dkv_k_ref, dkv_v_ref, dhb_ref, dz_ref, dh_ref, send_ref, keep_ref, fgain_ref, again_ref, hgain_ref,
     do_ref, dq_ref, delta_ref) = rest
    i = pl.program_id(0)
    core = core_ref[0]
    block = order.block(i, core)
    is_send = order.is_send(i, core)

    @pl.when(i == 0)
    def _():
        fgain_ref[...] = jnp.zeros_like(fgain_ref)
        again_ref[...] = jnp.zeros_like(again_ref)
        hgain_ref[...] = jnp.zeros_like(hgain_ref)
        if first:
            dkv_k_ref[...] = jnp.zeros_like(dkv_k_ref)
            dkv_v_ref[...] = jnp.zeros_like(dkv_v_ref)
        else:
            dkv_k_ref[...] = carried[0][...]
            dkv_v_ref[...] = carried[1][...]

    total = jnp.where(is_send, got_ref[...].astype(F32), own_ref[...].astype(F32))
    dxn = jnp.where(is_send, dgot_ref[...].astype(F32), down_ref[...].astype(F32))
    h = x_ref[...].astype(F32) + total
    rstd = lax.rsqrt(jnp.mean(h * h, axis=1, keepdims=True) + EPSILON)
    hhat = h * rstd
    fgain_ref[...] += jnp.sum(dxn * hhat, axis=0, keepdims=True)
    u = dxn * gain_ref[...]
    dh = g_ref[...].astype(F32) + rstd * (u - hhat * jnp.mean(u * hhat, axis=1, keepdims=True))
    dh_ref[...] = dh
    dhb = dh.astype(BF16)
    dhb_ref[...] = dhb
    dheads = dot(dhb, wo_ref[...]).astype(BF16).astype(F32)
    delta_t = (dheads * o_ref[...].astype(F32)).T
    for group in range(2):
        do_ref[group] = head_pads(dheads[:, group * 128:(group + 1) * 128], group)
        sums = [
            jnp.sum(delta_t[(2 * group + r) * HD:(2 * group + r + 1) * HD], axis=0, keepdims=True)
            for r in range(2)
        ]
        delta_ref[group:group + 1, :] = jnp.concatenate(sums, axis=1)
    dq_ref[...] = jnp.zeros_like(dq_ref)
    start = start_ref[0]
    key_place = lax.broadcasted_iota(jnp.int32, (BLK, 2 * BLK), 0)

    def step(kb, diagonal):
        at = pl.multiple_of(kb * BLK, BLK)
        keys = k_ref[pl.ds(at, BLK), :]
        values = v_ref[pl.ds(at, BLK), :]
        allowed = key_place >= start - at
        if diagonal:
            lane = lax.broadcasted_iota(jnp.int32, (BLK, 2 * BLK), 1)
            allowed = allowed & (key_place <= lax.rem(lane, BLK))
        dk = dkv_k_ref[pl.ds(at, BLK), :]
        dv = dkv_v_ref[pl.ds(at, BLK), :]
        for group in range(2):
            queries, douts = q_ref[0, group], do_ref[group]
            scores = dot_nt(keys, queries) * EXP2_SCALE - lse_ref[0, group:group + 1, :]
            probs = jnp.exp2(jnp.where(allowed, scores, BIG_NEGATIVE))
            dprobs = dot_nt(values, douts)
            dscores = (probs * (dprobs - delta_ref[group:group + 1, :])).astype(BF16)
            dv += dot(probs.astype(BF16), douts)
            dk += dot(dscores, queries)
            dq_ref[group] += dot(kt_ref[group * HD:(group + 1) * HD, pl.ds(at, BLK)], dscores)
        dkv_k_ref[pl.ds(at, BLK), :] = dk
        dkv_v_ref[pl.ds(at, BLK), :] = dv

    def loop_body(kb, carry):
        step(kb, False)
        return carry

    lax.fori_loop(lo_ref[block], block, loop_body, 0)
    step(block, True)

    parts = []
    for group in range(2):
        dq_t = dq_ref[group]
        parts += [dq_t[:, :BLK], dq_t[:, BLK:]]
    dq = jnp.concatenate(parts, axis=0).T * SCALE
    cos, sin = cos_ref[...], sin_ref[...]

    def post_back(grad, raw, gain):
        dn = grad * cos - swap_halves(grad) * sin
        rstd = lax.rsqrt(pair_mean(raw * raw) + EPSILON)
        hat = raw * rstd
        gain_grad = jnp.sum(dn * hat, axis=0, keepdims=True)
        dhat = dn * gain
        return rstd * (dhat - hat * pair_mean(dhat * hat)), gain_grad

    at = pl.multiple_of(block * BLK, BLK)
    qg = jnp.zeros((1, 128), F32)
    for group in range(2):
        lanes = slice(group * 128, (group + 1) * 128)
        dzq, gain_grad = post_back(dq[:, lanes], z_ref[:, lanes], qgain_ref[...])
        dz_ref[:, lanes] = dzq.astype(BF16)
        qg += gain_grad
    dzk, kg = post_back(dkv_k_ref[pl.ds(at, BLK), :] * SCALE, z_ref[:, 256:384], kgain_ref[...])
    dz_ref[:, 256:384] = dzk.astype(BF16)
    dz_ref[:, 384:512] = dkv_v_ref[pl.ds(at, BLK), :].astype(BF16)
    hgain_ref[0:1, :] += qg
    hgain_ref[1:2, :] += kg
    dxn_one = dot_nt(dz_ref[...], wqkv_ref[...]).astype(BF16)
    put(is_send, send_ref, keep_ref, dxn_one)
    x = x_ref[...].astype(F32)
    xhat = x * lax.rsqrt(jnp.mean(x * x, axis=1, keepdims=True) + EPSILON)
    again_ref[...] += jnp.sum(dxn_one.astype(F32) * xhat, axis=0, keepdims=True)


def back_call(chunk, half, core, lo, x, own, got, down, dgot, g, gain, q, k, v, kt, o, lse, start, w,
              z, cos, sin, qgain, kgain, carried, previous):
    seq, width = x.shape
    order = Order(chunk, half, True)
    row, local, send, keep = order_specs(order)
    first = len(previous) == 0
    n_prev = len(previous)
    rows = half * BLK
    by_block = lambda *tail: pl.BlockSpec((1,) + tail, lambda i, c, *s: (order.block(i, c[0]),) + (0,) * len(tail))
    n_in = 2 + 21
    extra = [] if first else [whole((seq, 128))] * 2 + [ANY] * n_prev
    return pl.pallas_call(
        functools.partial(back_kernel, order, n_prev, first),
        grid_spec=pltpu.PrefetchScalarGridSpec(
            num_scalar_prefetch=2,
            grid=(2 * half,),
            in_specs=[
                row(width), keep(width), send(width), keep(width), send(width), row(width), whole((1, width)),
                by_block(2, 2 * BLK, 128), whole((seq, 128)), whole((seq, 128)), whole((128, seq)),
                row(256), by_block(2, 2 * BLK), by_block(1, 2 * BLK),
                pl.BlockSpec((width, 256), lambda i, *s: (0, 2)),
                pl.BlockSpec((width, 512), lambda i, *s: (0, 0)),
                row(384), row(128), row(128), whole((1, 128)), whole((1, 128)),
            ] + extra,
            out_specs=[
                whole((seq, 128)), whole((seq, 128)), row(width), row(512), local(width),
                send(width), keep(width), whole((1, width)), whole((1, width)), whole((2, 128)),
            ],
            scratch_shapes=[
                pltpu.VMEM((2, 2 * BLK, 128), BF16),
                pltpu.VMEM((2, HD, 2 * BLK), F32),
                pltpu.VMEM((2, 2 * BLK), F32),
            ],
        ),
        out_shape=[
            sds((seq, 128), F32), sds((seq, 128), F32), sds((seq, width), BF16), sds((seq, 512), BF16),
            sds((2 * rows, width), F32), sds((rows, width), BF16), sds((rows, width), BF16),
            sds((1, width), F32), sds((1, width), F32), sds((2, 128), F32),
        ],
        input_output_aliases={n_in + 2 + j: 2 + j for j in range(n_prev)},
        compiler_params=params(),
        cost_estimate=cost(5 * 7.5 * 2 * half),
        name=f"back_{chunk}",
    )(core, lo, x, own, got, down, dgot, g, gain, q, k, v, kt, o, lse, start, w, w, z, cos, sin,
      qgain, kgain, *carried, *previous)


def input_kernel(order, n_prev, core_ref, dh_ref, x_ref, own_ref, got_ref, gain_ref, *rest):
    (out_ref,) = rest[n_prev:]
    i = pl.program_id(0)
    is_send = order.is_send(i, core_ref[0])
    dxn = jnp.where(is_send, got_ref[...].astype(F32), own_ref[...].astype(F32))
    x = x_ref[...].astype(F32)
    rstd = lax.rsqrt(jnp.mean(x * x, axis=1, keepdims=True) + EPSILON)
    xhat = x * rstd
    u = dxn * gain_ref[...]
    out_ref[...] = dh_ref[...] + rstd * (u - xhat * jnp.mean(u * xhat, axis=1, keepdims=True))


def input_call(chunk, half, core, dh, x, own, got, gain, previous):
    seq, width = x.shape
    order = Order(chunk, half, False)
    row, local, send, keep = order_specs(order)
    n_prev = len(previous)
    return pl.pallas_call(
        functools.partial(input_kernel, order, n_prev),
        grid_spec=pltpu.PrefetchScalarGridSpec(
            num_scalar_prefetch=1,
            grid=(2 * half,),
            in_specs=[local(width), row(width), keep(width), send(width), whole((1, width))] + [ANY] * n_prev,
            out_specs=[row(width)],
        ),
        out_shape=[sds((seq, width), F32)],
        input_output_aliases={6 + j: j for j in range(n_prev)},
        compiler_params=params(),
        cost_estimate=cost(5 * 2 * 2 * half),
        name=f"grad_input_{chunk}",
    )(core, dh, x, own, got, gain, *previous)


def output_kernel(core_ref, x_ref, *refs):
    (out_ref,) = refs[-1:]
    chunk = pl.program_id(0)
    mine = pl.program_id(1) == core_ref[0]
    for index in range(CHUNKS):
        own_ref, got_ref = refs[2 * index:2 * index + 2]
        yown_ref, ygot_ref = refs[2 * CHUNKS + 2 * (index // 2):2 * CHUNKS + 2 * (index // 2) + 2]
        for kept in range(2):
            @pl.when((chunk == index) & (mine if kept else jnp.logical_not(mine)))
            def _(a_ref=own_ref if kept else got_ref, y_ref=yown_ref if kept else ygot_ref):
                total = a_ref[...].astype(F32) + y_ref[...].astype(F32)
                out_ref[...] = (x_ref[...].astype(F32) + total).astype(BF16)


def output_call(half, core, x, attn_sums, y_sums):
    seq, width = x.shape
    rows = BLK
    per = half * BLK // rows
    row = pl.BlockSpec((rows, width), lambda c, h, i, *s: ((c * 2 + h) * per + i, 0))

    def moving(index):
        def at(c, h, i, *s):
            return (jnp.where(c == index, i, jnp.where(c < index, 0, per - 1)), 0)

        return pl.BlockSpec((rows, width), at)

    def y_moving(pair):
        def at(c, h, i, *s):
            here = lax.rem(c, 2) * per + i
            return (jnp.where(c // 2 == pair, here, jnp.where(c // 2 < pair, 0, 2 * per - 1)), 0)

        return pl.BlockSpec((rows, width), at)

    args, specs = [], []
    for index in range(CHUNKS):
        args += list(attn_sums[index])
        specs += [moving(index)] * 2
    for pair in range(CHUNKS // 2):
        args += list(y_sums[pair])
        specs += [y_moving(pair)] * 2
    return pl.pallas_call(
        output_kernel,
        grid_spec=pltpu.PrefetchScalarGridSpec(
            num_scalar_prefetch=1,
            grid=(CHUNKS, 2, per),
            in_specs=[row] + specs,
            out_specs=row,
        ),
        out_shape=sds((seq, width), BF16),
        compiler_params=pltpu.CompilerParams(
            dimension_semantics=("arbitrary",) * 3, vmem_limit_bytes=56 * 1024 * 1024
        ),
        cost_estimate=cost(5 * 8),
        name="output",
    )(core, x, *args)


def pack_kernel(wq_ref, wk_ref, wv_ref, wo_ref, gain_ref, wg_ref, wu_ref, wd_ref, attn_ref, ffn_ref):
    queries, keys = wq_ref.shape[1], wk_ref.shape[1]
    hidden = wg_ref.shape[1]
    attn_ref[:, :queries] = wq_ref[...]
    attn_ref[:, queries:queries + keys] = wk_ref[...]
    attn_ref[:, queries + keys:queries + 2 * keys] = wv_ref[...]
    at = queries + 2 * keys
    attn_ref[:, at:at + queries] = wo_ref[...].astype(F32).T.astype(BF16)
    attn_ref[:, at + queries:] = gain_ref[...].astype(F32).T.astype(BF16)
    ffn_ref[:, :hidden] = wg_ref[...]
    ffn_ref[:, hidden:2 * hidden] = wu_ref[...]
    ffn_ref[:, 2 * hidden:] = wd_ref[...].astype(F32).T.astype(BF16)


def pack(w_query, w_key, w_value, w_out, attn_gain, ffn_gain, w_gate, w_up, w_down):
    shard = w_query.shape[0]
    if shard % 128:
        gains = jnp.stack([attn_gain, ffn_gain] + [jnp.zeros_like(attn_gain)] * 126, axis=1)
        return (
            jnp.concatenate([w_query, w_key, w_value, w_out.T, gains], axis=1),
            jnp.concatenate([w_gate, w_up, w_down.T], axis=1),
        )
    gains = jnp.concatenate([attn_gain[None], ffn_gain[None], jnp.zeros((126, shard), BF16)], axis=0)
    columns = 2 * w_query.shape[1] + 2 * w_key.shape[1] + 128
    return pl.pallas_call(
        pack_kernel,
        out_shape=[sds((shard, columns), BF16), sds((shard, 3 * w_gate.shape[1]), BF16)],
        cost_estimate=cost(3),
        name="pack",
    )(w_query, w_key, w_value, w_out, gains, w_gate, w_up, w_down)


def dp_place(n_dp):
    at = lax.axis_index("dp")
    return at // 2, lax.rem(at, 2)


def ring_of(n_dp):
    return [(i, (i + 2) % n_dp) for i in range(n_dp)]


PAIR = [(i, i ^ 1) for i in range(8)]


def place_kernel(at_ref, *refs):
    pieces, out_ref = refs[:8], refs[8]
    i = pl.program_id(0)
    step = lax.rem(at_ref[0] + 4 - i // 2, 4)
    same = lax.rem(i, 2) == at_ref[1]
    for index in range(4):
        for own in range(2):
            @pl.when((step == index) & (same if own else jnp.logical_not(same)))
            def _(ref=pieces[index + 4 * (1 - own)]):
                out_ref[...] = ref[...]


def place_pieces(line, other, z, y):
    rows, columns = line[0].shape
    return pl.pallas_call(
        place_kernel,
        grid_spec=pltpu.PrefetchScalarGridSpec(
            num_scalar_prefetch=1,
            grid=(8,),
            in_specs=[
                pl.BlockSpec((rows, columns), lambda i, *s: (0, 0), pipeline_mode=pl.Buffered(1))
            ] * 8,
            out_specs=pl.BlockSpec((rows, columns), lambda i, *s: (i, 0)),
        ),
        out_shape=sds((8 * rows, columns), line[0].dtype),
        compiler_params=params(),
        cost_estimate=cost(0.2),
        name="place_pieces",
    )(jnp.stack([z, y]).astype(jnp.int32), *line, *other)


class Gather:
    def __init__(self, piece, n_dp, *clear):
        self.n_dp, self.piece, self.line, self.other = n_dp, piece, [], []
        if n_dp == 8:
            self.step(piece, *clear)

    def step(self, piece, *clear):
        self.line.append(piece)
        self.other.append(lax.ppermute(after(piece, *clear) if clear else piece, "dp", PAIR))

    def relay(self, *ahead):
        if self.n_dp == 8:
            piece = self.line[-1]
            if len(self.line) > 1:
                piece = after(piece, self.other[-2])
            piece = lax.ppermute(piece, "dp", ring_of(8))
            self.step(after(piece, *ahead) if ahead else piece)
            return self.line[-1]
        return self.piece

    def crossed(self, at):
        return self.other[at] if self.n_dp == 8 else self.piece

    def result(self, turn=None):
        if self.n_dp != 8:
            return lax.all_gather(self.piece, "dp", axis=0, tiled=True)
        z, y = dp_place(8)
        if turn is not None:
            z = after(z, turn)
        return place_pieces(self.line, self.other, z, y)


class Lane:
    def __init__(self, steps):
        self.steps, self.waits = steps, None
        self.move(None)

    def move(self, values):
        try:
            self.waits = self.steps.send(values)
        except StopIteration:
            self.waits = None


def advance(token, lanes, *extra):
    lanes = [lane for lane in lanes if lane.waits is not None]
    values, token, _ = lax.optimization_barrier(([lane.waits for lane in lanes], token, extra))
    for lane, value in zip(lanes, values):
        lane.move(value)
    return token


def scatter(grad, n_dp, store, key, crossings):
    if n_dp != 8:
        store[key] = lax.psum_scatter(grad, "dp", scatter_dimension=0, tiled=True).astype(F32)
        crossings += [grad] * 2
        return
    z, y = dp_place(n_dp)
    rows, columns = grad.shape[0] // n_dp, grad.shape[1]

    def part(step, line):
        at = (lax.rem(z + 4 - step, 4) * 2 + line) * rows
        return lax.dynamic_slice(grad, (at, 0), (rows, columns))

    kept = [part(step, y) for step in (1, 2, 3, 4)]
    for step in (1, 3):
        parts = jnp.concatenate([part(step, 1 - y), part(step + 1, 1 - y)], axis=0)
        crossings.append(lax.ppermute(parts, "dp", PAIR))
    passed = ()
    for step in range(4):
        crossed, *values = yield (crossings[step // 2],) + passed
        total = kept[step].astype(F32)
        for value in [crossed[step % 2 * rows:(step % 2 + 1) * rows]] + values:
            total = total + value.astype(F32)
        if step < 3:
            passed = (lax.ppermute(total.astype(BF16), "dp", ring_of(8)),)
    store[key] = total


NEAR = [(t, t ^ 1) for t in range(4)]
FAR = [(t, t ^ 2) for t in range(4)]


def sum_tensor(send, keep, store, key):
    (got,) = yield (lax.ppermute(send, "tensor", NEAR),)
    mine = (keep.astype(F32) + got.astype(F32)).astype(BF16)
    (got,) = yield (lax.ppermute(mine, "tensor", FAR),)
    own = (mine.astype(F32) + got.astype(F32)).astype(BF16)
    (got,) = yield (lax.ppermute(own, "tensor", NEAR),)
    store[key] = (own, got)


def sum_all(value, n_dp, store, key):
    for axis, size in (("tensor", 4), ("dp", n_dp)):
        bit = 1
        while bit < size:
            (got,) = yield (lax.ppermute(value, axis, [(i, i ^ bit) for i in range(size)]),)
            value = value + got
            bit *= 2
    store[key] = value


def body(
    tokens, segment_ids, positions, pad_mask, w_query, w_key, w_value, w_out, w_gate, w_up, w_down,
    attn_gain, ffn_gain, query_gain, key_gain, cotangent,
):
    del segment_ids
    seq, width = tokens.shape
    shard = w_query.shape[0]
    n_dp = width // shard
    hidden = w_gate.shape[1]
    chunks = CHUNKS
    half = seq // chunks // 2 // BLK
    blocks = seq // BLK
    core_id = lax.rem(lax.axis_index("tensor"), 2).astype(jnp.int32).reshape(1)

    place = jnp.arange(seq, dtype=jnp.int32)
    start = jnp.where(pad_mask == 1, place - positions, place)
    lo = (place[::BLK] - positions[::BLK]) // BLK
    start_rows = jnp.tile(start.reshape(blocks, 1, BLK), (1, 1, 2))
    half_size = HD // 2
    inverse = THETA ** (-(jnp.arange(half_size).astype(F32) * 2.0 / HD))
    angles = positions.astype(F32)[:, None] * inverse[None, :]
    cos_half, sin_half = jnp.cos(angles), jnp.sin(angles)
    cos = jnp.concatenate([cos_half] * 4, axis=1)
    sin = jnp.concatenate([-sin_half, sin_half] * 2, axis=1)

    attn_piece, ffn_piece = pack(
        w_query, w_key, w_value, w_out, attn_gain, ffn_gain, w_gate, w_up, w_down
    )
    gather_attn = Gather(attn_piece, n_dp)
    gather_attn.relay()
    gather_attn.relay(cos, sin)
    late = gather_attn.relay()
    w_attn = gather_attn.result()
    gather_ffn = Gather(after(ffn_piece, late), n_dp, *gather_attn.other)
    gain_rows = w_attn[:, 768:770].T.astype(F32)
    attn_scales, ffn_scales = gain_rows[0:1], gain_rows[1:2]
    query_scales = jnp.tile(query_gain.astype(F32), 2)[None]
    key_scales = jnp.tile(key_gain.astype(F32), 2)[None]

    line_one = gather_ffn.relay(w_attn)
    xn_one, z, q, k, v, kt, vt = qkv_call(
        tokens, attn_scales, w_attn, cos, sin, query_scales, key_scales
    )
    order = list(range(chunks))[::-1]
    previous = ()
    attn_sum, ffn_grad_sum, y_sums, input_grad_sum, dhs, totals = {}, {}, {}, {}, {}, {}
    lanes = []
    for step, c in enumerate(order):
        turn = core_id
        if step == 0:
            turn = after(turn, line_one)
            line_two = gather_ffn.relay()
        if step == 1:
            turn = after(turn, line_two, gather_ffn.crossed(0))
            line_three = gather_ffn.relay()
        if step == 2:
            turn = advance(turn, [lanes[0]], gather_ffn.crossed(1))
        if step == 3:
            turn = advance(turn, [lanes[1]])
        heads, lse, send, keep = attn_call(c, half, turn, lo, q, k, vt, start_rows, w_attn, previous)
        previous = (heads, lse)
        lanes.append(Lane(sum_tensor(send, keep, attn_sum, c)))
    turn = advance(core_id, [lanes[0], lanes[2], lanes[3]], line_three, gather_ffn.crossed(2))
    turn = advance(turn, [lanes[0], lanes[1]], gather_ffn.crossed(3))
    w_ffn = gather_ffn.result(turn)
    late = lanes
    previous, y_previous = (), ()
    lanes, y_lanes = [], []
    for step, c in enumerate(order):
        if step == 1:
            turn = advance(after(core_id, dsend), late[1:3])
        if step == 2:
            turn = advance(after(core_id, dsend), late[2:4] + [lanes[0]])
        if step == 3:
            turn = advance(after(core_id, dsend), [late[3], lanes[0], lanes[1]])
        own, got = attn_sum[c]
        xn_two, dgu, hid, dsend, dkeep, ysend, ykeep = ffn_call(
            c, half, turn, tokens, own, got, cotangent, ffn_scales, w_ffn, previous, y_previous
        )
        previous = (xn_two, dgu, hid)
        y_previous = (ysend, ykeep) if c % 2 else ()
        lanes.append(Lane(sum_tensor(dsend, dkeep, ffn_grad_sum, c)))
        if c % 2 == 0:
            y_lanes.append(Lane(sum_tensor(ysend, ykeep, y_sums, c // 2)))
    tn = (((0,), (0,)), ((), ()))
    turn = advance(after(core_id, dsend), lanes[:3])
    hid = after(hid, turn)
    grad_down_t = lax.dot_general(cotangent, hid, tn, preferred_element_type=F32).astype(BF16)
    down_got, gate_up_got, attn_got = [], [], []
    down_lane = Lane(scatter(grad_down_t, n_dp, totals, "down", down_got))
    turn = advance(after(core_id, grad_down_t), lanes[1:4])
    dgu = after(dgu, turn)
    grad_gate_up = lax.dot_general(xn_two, dgu, tn, preferred_element_type=F32).astype(BF16)
    gate_up_lane = Lane(scatter(grad_gate_up, n_dp, totals, "gate_up", gate_up_got))

    previous, carried = (), ()
    ffn_gain_grad = jnp.zeros((1, width), F32)
    attn_gain_grad = jnp.zeros((1, width), F32)
    head_gain_grad = jnp.zeros((2, 128), F32)
    back_lanes = []
    for step, c in enumerate(order):
        if step == 0:
            turn = advance(
                after(core_id, grad_gate_up), [lanes[2], y_lanes[0], down_lane], *down_got[:1]
            )
        if step == 1:
            turn = advance(after(core_id, hg), [lanes[3], y_lanes[1], down_lane], *down_got)
        if step == 2:
            turn = advance(
                after(core_id, hg), [lanes[3], y_lanes[0], back_lanes[0], down_lane, gate_up_lane]
            )
        if step == 3:
            turn = advance(
                after(core_id, hg), y_lanes + [back_lanes[0], back_lanes[1], down_lane, gate_up_lane]
            )
        own, got = attn_sum[c]
        down, dgot = ffn_grad_sum[c]
        dk, dv, dhb, dz, dhs[c], send, keep, fg, ag, hg = back_call(
            c, half, turn, lo, tokens, own, got, down, dgot, cotangent, ffn_scales, q, k, v, kt,
            heads, lse, start_rows, w_attn, z, cos, sin, query_scales, key_scales, carried, previous,
        )
        carried, previous = (dk, dv), (dhb, dz)
        ffn_gain_grad += fg
        attn_gain_grad += ag
        head_gain_grad += hg
        back_lanes.append(Lane(sum_tensor(send, keep, input_grad_sum, c)))

    turn = advance(after(core_id, hg), back_lanes[:3] + [y_lanes[1]])
    head_gains = head_gain_grad[:, :HD] + head_gain_grad[:, HD:]
    small = jnp.concatenate(
        [attn_gain_grad.reshape(-1), 0.25 * ffn_gain_grad.reshape(-1), head_gains.reshape(-1)]
    )
    small_lane = Lane(sum_all(small.reshape(-1, 128), n_dp, totals, "small"))
    dz = after(dz, turn)
    grad_qkv = lax.dot_general(xn_one, dz, tn, preferred_element_type=F32).astype(BF16)
    grad_out_t = lax.dot_general(dhb, heads, tn, preferred_element_type=F32).astype(BF16)
    grad_attn = jnp.concatenate([grad_qkv, grad_out_t], axis=1)
    attn_lane = Lane(scatter(grad_attn, n_dp, totals, "attn", attn_got))
    turn = advance(after(core_id, grad_attn), [back_lanes[3], small_lane])
    output = output_call(half, turn, tokens, attn_sum, y_sums)
    turn = advance(
        after(core_id, output), [attn_lane, back_lanes[1], back_lanes[2], small_lane, gate_up_lane], *attn_got
    )

    previous_in = ()
    for step, c in enumerate(order):
        if step == 2:
            turn = advance(after(core_id, grad_input), [attn_lane, back_lanes[2], back_lanes[3], small_lane])
        if step == 3:
            turn = advance(after(core_id, grad_input), [attn_lane, back_lanes[3], small_lane])
        eown, egot = input_grad_sum[c]
        (grad_input,) = input_call(c, half, turn, dhs[c], tokens, eown, egot, attn_scales, previous_in)
        previous_in = (grad_input,)
    last = [attn_lane, small_lane, gate_up_lane]
    while any(lane.waits is not None for lane in last):
        turn = advance(turn, last)
    down_own, gate_up_own, attn_own = totals["down"], totals["gate_up"], totals["attn"]
    small = totals["small"].reshape(-1)
    mine = lax.axis_index("dp") * shard
    grad_attn_gain = lax.dynamic_slice(small, (mine,), (shard,))
    grad_ffn_gain = lax.dynamic_slice(small, (width + mine,), (shard,))
    return (
        output,
        grad_input,
        attn_own[:, :256],
        attn_own[:, 256:384],
        attn_own[:, 384:512],
        attn_own[:, 512:768].T,
        gate_up_own[:, :hidden],
        gate_up_own[:, hidden:],
        down_own.T,
        grad_attn_gain,
        grad_ffn_gain,
        small[2 * width:2 * width + HD],
        small[2 * width + HD:],
    )


def solution(mesh):
    rows, flat, both = P("dp", None), P("dp"), P("dp", "tensor")
    columns = P("tensor", "dp")
    return jax.shard_map(
        body,
        mesh=mesh,
        in_specs=(
            rows, flat, flat, flat, both, both, both, columns, both, both, columns, flat, flat, P(), P(), rows,
        ),
        out_specs=(rows, rows, both, both, both, columns, both, both, columns, flat, flat, P(), P()),
        check_vma=False,
    )
```
